256 devices in a mesh: tm: 32 (over z, y), slab: 8 (over x, core).
Axes of the slice: x: 4, y: 4, z: 8, core: 2. Of those that a mesh axis runs over, the one named last changes fastest.
Arguments:
- features: bfloat16 [32, 12288, 256], P('tm', 'slab'), may hold values from -6 to 6
- ref_lists: int32 [32, 8, 32], P('tm'), may hold values from 0 to 11
- tile_rows: int32 [32, 256], P('tm', 'slab'), may hold values from 0 to 11
- tile_sources: int32 [32, 256], P('tm', 'slab'), may hold values from 0 to 31
- tile_counts: int32 [32, 8], P('tm', 'slab'), may hold values from 9 to 32
- tile_values: bfloat16 [32, 256, 128, 128], P('tm', 'slab'), may hold values from -0.3125 to 0.3125
- w_input: bfloat16 [2, 256, 1024], replicated, may hold values from -0.375 to 0.375
- w_hidden: bfloat16 [2, 256, 1024], replicated, may hold values from -0.375 to 0.375
- bias: float32 [2, 1024], replicated, may hold values from -4 to 4
Outputs:
- hidden_out: bfloat16 [32, 12288, 256], P('tm', 'slab')
The draws below stay inside these ranges and needn't reach their ends.
Inputs may be any that keep to these rules, and one draw needn't show every extreme that they name: `ref_lists`: row tile indices within a slab. `tile_counts`: slots at or after the count are ignored.
All inputs are finite; a program needn't handle non-finite values.
Results may differ from the reference program's by a relative error of at most 0.0055.
Values may be sent and summed in bfloat16 or wider, within the bound.
A program may use at most 64 MiB of HBM per device.

```python
import jax
import jax.numpy as jnp
from jax import lax

F = 256
H = 256
TILE = 128
ROWS = 1536
REFS = 4
LAYERS = 2
MAXT = 32
TIMES = 32
NODES = 12288
N_SLAB = 8


def place_ends(result, rng, least, top_value):
    dims = result.shape
    spot = [jax.random.randint(jax.random.fold_in(rng, axis), (), 0, dims[axis]) for axis in range(len(dims))]
    result = result.at[tuple(spot)].set(least)
    longest = dims.index(max(dims))
    spot[longest] = (spot[longest] + 1) % dims[longest]
    return result.at[tuple(spot)].set(top_value)


def block_levels(stream_key, extent, pieces, low, high):
    level = 1.0
    for axis_at, parts in pieces:
        steps = jax.random.uniform(jax.random.fold_in(jax.random.fold_in(stream_key, 6), axis_at), (parts,), jnp.float32, low / len(pieces), high / len(pieces))
        level = level * jnp.repeat(jnp.exp(steps), extent[axis_at] // parts).reshape((-1,) + (1,) * (len(extent) - 1 - axis_at))
    return level


def gaussian(own_key, shape, width, limit, pieces=(), kind=jnp.bfloat16):
    drawn = jax.random.normal(own_key, shape, jnp.float32) * width
    if len(pieces) > 0:
        drawn = block_levels(own_key, shape, pieces, -0.22, 0.18) * drawn
    return jnp.clip(drawn, min=-limit, max=limit).astype(kind)


def setup_inputs(seed: int = 0) -> dict:
    seeds = jax.random.split(jax.random.key(seed), 10)
    features = gaussian(seeds[0], (TIMES, NODES, F), 1.0, 6.0, ((0, 32), (1, 8)))
    ref_lists = place_ends(jax.random.randint(seeds[1], (TIMES, N_SLAB, N_SLAB * REFS), 0, ROWS // TILE), jax.random.fold_in(seeds[1], 1), 0, (ROWS // TILE) - 1).astype(jnp.int32)
    tile_rows = place_ends(jax.random.randint(seeds[2], (TIMES, N_SLAB * MAXT), 0, ROWS // TILE), jax.random.fold_in(seeds[2], 1), 0, (ROWS // TILE) - 1).astype(jnp.int32)
    tile_sources = place_ends(jax.random.randint(seeds[3], (TIMES, N_SLAB * MAXT), 0, N_SLAB * REFS), jax.random.fold_in(seeds[3], 1), 0, (N_SLAB * REFS) - 1).astype(jnp.int32)
    tile_counts = place_ends(jax.random.randint(seeds[4], (TIMES, N_SLAB), MAXT // 4 + 1, MAXT + 1), jax.random.fold_in(seeds[4], 1), MAXT // 4 + 1, MAXT).astype(jnp.int32)
    tile_values = gaussian(seeds[5], (TIMES, N_SLAB * MAXT, TILE, TILE), (3 * TILE) ** -0.5, 0.3125, ((0, 32), (1, 8)))
    w_input = gaussian(seeds[6], (LAYERS, F, 4 * H), F ** -0.5, 0.375)
    w_hidden = gaussian(seeds[7], (LAYERS, H, 4 * H), H ** -0.5, 0.375)
    bias = gaussian(seeds[8], (LAYERS, 4 * H), 1.0, 4.0, (), jnp.float32)
    return {"features": features, "ref_lists": ref_lists, "tile_rows": tile_rows, "tile_sources": tile_sources, "tile_counts": tile_counts, "tile_values": tile_values, "w_input": w_input, "w_hidden": w_hidden, "bias": bias}


def lstm_run(inputs, weight_in, weight_rec, gate_bias):
    steps_count, vertex_count, feature_width = inputs.shape
    projected = jnp.dot(inputs.reshape(-1, feature_width), weight_in, preferred_element_type=jnp.float32)
    projected = projected.reshape(steps_count, vertex_count, -1) + gate_bias
    unit_count = weight_rec.shape[0]

    def advance(state, gate_input):
        hidden, memory = state
        gate_sum = gate_input + jnp.dot(hidden, weight_rec, preferred_element_type=jnp.float32)
        in_gate, forget, candidate, out_gate = jnp.split(gate_sum, 4, axis=-1)
        memory = jax.nn.sigmoid(forget) * memory + jax.nn.sigmoid(in_gate) * jnp.tanh(candidate)
        hidden = (jax.nn.sigmoid(out_gate) * jnp.tanh(memory)).astype(jnp.bfloat16)
        return (hidden, memory), hidden

    start_state = (jnp.zeros((vertex_count, unit_count), jnp.bfloat16), jnp.zeros((vertex_count, unit_count), jnp.float32))
    final_state, outputs = lax.scan(advance, start_state, projected, unroll=4)
    return outputs


def convolve(snapshot):
    current, ref_table, row_list, source_list, count_list, weight_tiles = snapshot
    row_tiles = ROWS // TILE
    tiles = current.reshape(N_SLAB * row_tiles, TILE, -1)
    offsets = jnp.arange(N_SLAB * REFS, dtype=jnp.int32) // REFS * row_tiles
    global_table = ref_table + offsets[None, :]
    sources = source_list.reshape(N_SLAB, MAXT)
    global_index = jnp.take_along_axis(global_table, sources, axis=1)
    picked = jnp.take(tiles, global_index.reshape(-1), axis=0).reshape(N_SLAB, MAXT, TILE, -1)
    weights = weight_tiles.reshape(N_SLAB, MAXT, TILE, TILE)
    products = jnp.einsum("pkij,pkjf->pkif", weights.astype(jnp.float32), picked.astype(jnp.float32))
    live = jnp.arange(MAXT, dtype=jnp.int32)[None, :] < count_list[:, None]
    targets = row_list.reshape(N_SLAB, MAXT)
    one_hot = (targets[:, None, :] == jnp.arange(row_tiles, dtype=jnp.int32)[None, :, None]) & live[:, None, :]
    mixed = jnp.einsum("prk,pkif->prif", one_hot.astype(jnp.float32), products)
    return mixed.reshape(NODES, -1).astype(jnp.bfloat16)


def reference(features, ref_lists, tile_rows, tile_sources, tile_counts, tile_values, w_input, w_hidden, bias):
    current = features
    for layer_index in range(LAYERS):
        mixed = lax.map(convolve, (current, ref_lists, tile_rows, tile_sources, tile_counts, tile_values))
        blocks = mixed.reshape(TIMES, N_SLAB, ROWS, -1).transpose(1, 0, 2, 3)

        def run_block(block_rows):
            return lstm_run(block_rows, w_input[layer_index], w_hidden[layer_index], bias[layer_index])

        states = lax.map(run_block, blocks)
        current = states.transpose(1, 0, 2, 3).reshape(TIMES, NODES, -1)
    return current
```

```python
import functools

import jax
import jax.numpy as jnp
from jax import lax
from jax.experimental import pallas as pl
from jax.experimental.pallas import tpu as pltpu
from jax.sharding import PartitionSpec as P

CHUNKS = (16, 32)


def sigmoid(x):
    return 0.5 * jnp.tanh(0.5 * x) + 0.5


def kernel(
    times, slabs, refs, tile, slots, units,
    table, features, values_hbm, w_in_hbm, w_rec_hbm, bias,
    out,
    values, w_in, w_rec, pack, arrived_first, arrived_next, sums, mixed, inputs, hidden, current, gates,
    load_sem, slab_sem, ahead_sem, back_sem,
):
    time, slab = lax.axis_index("tm"), lax.axis_index("slab")
    row_tiles = features.shape[0]
    layers = w_in.shape[0]
    starts = [times * sum(CHUNKS[:n]) for n in range(len(CHUNKS))]
    at_order, at_source, at_keep, at_last, at_filled, at_wanted = (
        0, slots, 2 * slots, 3 * slots, 3 * slots + row_tiles, 3 * slots + 2 * row_tiles,
    )

    loads = [
        pltpu.make_async_copy(values_hbm, values, load_sem.at[0]),
        pltpu.make_async_copy(w_in_hbm, w_in, load_sem.at[1]),
        pltpu.make_async_copy(w_rec_hbm, w_rec, load_sem.at[2]),
    ]
    for load in loads:
        load.start()

    barrier = pltpu.get_barrier_semaphore()

    @pl.loop(1, slabs)
    def _(step):
        pl.semaphore_signal(barrier, device_id={"slab": lax.rem(slab + step, slabs)})

    @pl.loop(1, times)
    def _(step):
        pl.semaphore_signal(barrier, device_id={"tm": lax.rem(time + step, times)})

    pl.semaphore_wait(barrier, slabs - 1 + times - 1)

    def bulk_wait(ref, sem):
        pltpu.make_async_copy(ref, ref, sem).wait()

    for layer in range(layers):
        here = features if layer == 0 else current
        after = out if layer == layers - 1 else current
        arrived = arrived_first if layer % 2 == 0 else arrived_next

        def pack_for(q, target, layer=layer, here=here):
            for j in range(refs):
                target[j] = here[table[at_wanted + q * refs + j]]

        @pl.loop(1, slabs)
        def _(step, layer=layer, pack_for=pack_for, arrived=arrived):
            q = lax.rem(slab + step, slabs)
            pack_for(q, pack.at[layer, q])
            pltpu.make_async_remote_copy(
                src_ref=pack.at[layer, q],
                dst_ref=arrived.at[pl.ds(slab * refs, refs)],
                send_sem=slab_sem.at[layer, 0],
                recv_sem=slab_sem.at[layer, 1],
                device_id={"slab": q},
            ).start()

        pack_for(slab, arrived.at[pl.ds(slab * refs, refs)])
        if layer == 0:
            loads[0].wait()
        bulk_wait(pack.at[layer, pl.ds(0, slabs - 1)], slab_sem.at[layer, 1])

        def add_slot(n, total, arrived=arrived):
            product = jnp.dot(
                values[table[at_order + n]],
                arrived[table[at_source + n]],
                preferred_element_type=jnp.float32,
            )
            total = total * table[at_keep + n].astype(jnp.float32) + product
            sums[n] = total
            return total

        lax.fori_loop(0, slots, add_slot, jnp.zeros((tile, units), jnp.float32))
        for r in range(row_tiles):
            filled = table[at_filled + r].astype(jnp.float32)
            mixed[layer, r * tile : (r + 1) * tile, :] = (
                sums[table[at_last + r]] * filled
            ).astype(jnp.bfloat16)

        for n, (size, start) in enumerate(zip(CHUNKS, starts)):

            @pl.loop(1, times)
            def _(step, n=n, size=size, start=start, layer=layer):
                peer = lax.rem(time + step, times)
                pltpu.make_async_remote_copy(
                    src_ref=mixed.at[layer, pl.ds(start + peer * size, size)],
                    dst_ref=inputs.at[layer, pl.ds(start + time * size, size)],
                    send_sem=ahead_sem.at[layer, n, 0],
                    recv_sem=ahead_sem.at[layer, n, 1],
                    device_id={"tm": peer},
                ).start()

            own = pl.ds(pl.multiple_of(start + time * size, size), size)
            inputs[layer, own, :] = mixed[layer, own, :]

        if layer == 0:
            loads[1].wait()
            loads[2].wait()

        for n, (size, start) in enumerate(zip(CHUNKS, starts)):
            most = (times - 1) * size
            bulk_wait(inputs.at[layer, pl.ds(start, most)], ahead_sem.at[layer, n, 1])

            block = 8 * size

            @pl.loop(0, times // 8)
            def _(m, start=start, block=block, layer=layer):
                part = pl.ds(pl.multiple_of(start + m * block, block), block)
                gates[part, :] = (
                    jnp.dot(inputs[layer, part, :], w_in[layer], preferred_element_type=jnp.float32)
                    + bias[layer : layer + 1, :]
                )

            def advance(t, state, size=size, start=start, layer=layer):
                last, memory = state
                part = pl.ds(pl.multiple_of(start + t * size, size), size)
                total = gates[part, :] + jnp.dot(
                    last, w_rec[layer], preferred_element_type=jnp.float32
                )
                in_gate, forget, candidate, out_gate = (
                    total[:, k * units : (k + 1) * units] for k in range(4)
                )
                memory = sigmoid(forget) * memory + sigmoid(in_gate) * jnp.tanh(candidate)
                last = (sigmoid(out_gate) * jnp.tanh(memory)).astype(jnp.bfloat16)
                hidden[layer, part, :] = last
                return last, memory

            lax.fori_loop(
                0, times, advance,
                (jnp.zeros((size, units), jnp.bfloat16), jnp.zeros((size, units), jnp.float32)),
            )

            home = (start + time * size) // tile
            place = pl.ds(pl.multiple_of(lax.rem(start + time * size, tile), size), size)

            @pl.loop(1, times)
            def _(step, n=n, size=size, start=start, layer=layer, after=after, home=home, place=place):
                peer = lax.rem(time + step, times)
                pltpu.make_async_remote_copy(
                    src_ref=hidden.at[layer, pl.ds(start + peer * size, size)],
                    dst_ref=after.at[home, place],
                    send_sem=back_sem.at[layer, n, 0],
                    recv_sem=back_sem.at[layer, n, 1],
                    device_id={"tm": peer},
                ).start()

            own = pl.ds(pl.multiple_of(start + time * size, size), size)
            after[home, place, :] = hidden[layer, own, :]

        for n, (size, start) in enumerate(zip(CHUNKS, starts)):
            most = (times - 1) * size
            bulk_wait(hidden.at[layer, pl.ds(start, most)], back_sem.at[layer, n, 1])

    for layer in range(layers):
        bulk_wait(pack.at[layer, pl.ds(0, slabs - 1)], slab_sem.at[layer, 0])
        for n, (size, start) in enumerate(zip(CHUNKS, starts)):
            most = (times - 1) * size
            bulk_wait(mixed.at[layer, pl.ds(start, most)], ahead_sem.at[layer, n, 0])
            bulk_wait(hidden.at[layer, pl.ds(start, most)], back_sem.at[layer, n, 0])


def slot_table(wanted, rows, sources, count, row_tiles):
    slots = rows.shape[0]
    index = jnp.arange(slots, dtype=jnp.int32)
    key = jnp.where(index < count, rows, row_tiles)
    before = (key[None, :] < key[:, None]) | (
        (key[None, :] == key[:, None]) & (index[None, :] < index[:, None])
    )
    rank = jnp.sum(before.astype(jnp.int32), axis=1)
    place = (rank[None, :] == index[:, None]).astype(jnp.int32)
    order = jnp.sum(place * index[None, :], axis=1)
    source = jnp.sum(place * sources[None, :], axis=1)
    sorted_key = jnp.sum(place * key[None, :], axis=1)
    keep = jnp.concatenate(
        [jnp.zeros((1,), jnp.int32), (sorted_key[1:] == sorted_key[:-1]).astype(jnp.int32)]
    )
    tiles = jnp.arange(row_tiles, dtype=jnp.int32)[:, None]
    last = jnp.maximum(jnp.sum((key[None, :] <= tiles).astype(jnp.int32), axis=1) - 1, 0)
    filled = jnp.any(key[None, :] == tiles, axis=1).astype(jnp.int32)
    return jnp.concatenate([order, source, keep, last, filled, wanted])


def local(
    features, ref_lists, tile_rows, tile_sources, tile_counts, tile_values, w_input, w_hidden, bias
):
    _, rows, width = features.shape
    _, slots, tile, _ = tile_values.shape
    layers, units = w_hidden.shape[:2]
    slabs, times = lax.axis_size("slab"), lax.axis_size("tm")
    refs = ref_lists.shape[2] // slabs
    wanted = lax.dynamic_slice_in_dim(ref_lists[0], lax.axis_index("slab") * refs, refs, 1)
    table = slot_table(
        wanted.reshape(-1), tile_rows[0], tile_sources[0], tile_counts[0, 0], rows // tile
    )
    vmem = pl.BlockSpec(memory_space=pltpu.VMEM)
    anywhere = pl.BlockSpec(memory_space=pl.ANY)
    parts = len(CHUNKS)
    result = pl.pallas_call(
        functools.partial(kernel, times, slabs, refs, tile, slots, units),
        out_shape=jax.ShapeDtypeStruct((rows // tile, tile, units), jnp.bfloat16),
        in_specs=[
            pl.BlockSpec(memory_space=pltpu.SMEM), vmem, anywhere, anywhere, anywhere, vmem,
        ],
        out_specs=vmem,
        scratch_shapes=[
            pltpu.VMEM(tile_values.shape[1:], jnp.bfloat16),
            pltpu.VMEM(w_input.shape, jnp.bfloat16),
            pltpu.VMEM(w_hidden.shape, jnp.bfloat16),
            pltpu.VMEM((layers, slabs, refs, tile, width), jnp.bfloat16),
            pltpu.VMEM((slabs * refs, tile, width), jnp.bfloat16),
            pltpu.VMEM((slabs * refs, tile, width), jnp.bfloat16),
            pltpu.VMEM((slots, tile, width), jnp.float32),
            pltpu.VMEM((layers, rows, width), jnp.bfloat16),
            pltpu.VMEM((layers, rows, width), jnp.bfloat16),
            pltpu.VMEM((layers, rows, units), jnp.bfloat16),
            pltpu.VMEM((rows // tile, tile, units), jnp.bfloat16),
            pltpu.VMEM((rows, 4 * units), jnp.float32),
            pltpu.SemaphoreType.DMA((3,)),
            pltpu.SemaphoreType.DMA((layers, 2)),
            pltpu.SemaphoreType.DMA((layers, parts, 2)),
            pltpu.SemaphoreType.DMA((layers, parts, 2)),
        ],
        compiler_params=pltpu.CompilerParams(
            collective_id=0, has_side_effects=True, vmem_limit_bytes=56 << 20
        ),
    )(table, features[0].reshape(rows // tile, tile, width), tile_values[0], w_input, w_hidden, bias)
    return result.reshape(1, rows, units)


def solution(mesh):
    in_specs = (
        P("tm", "slab", None),
        P("tm", None, None),
        P("tm", "slab"),
        P("tm", "slab"),
        P("tm", "slab"),
        P("tm", "slab", None, None),
        P(),
        P(),
        P(),
    )
    out_specs = P("tm", "slab", None)
    return jax.shard_map(local, mesh=mesh, in_specs=in_specs, out_specs=out_specs, check_vma=False)
```

```python
import functools

import jax
import jax.numpy as jnp
from jax import lax
from jax.experimental import pallas as pl
from jax.experimental.pallas import tpu as pltpu
from jax.sharding import PartitionSpec as P

CHUNKS = (16, 32)
LANES = 128


def sigmoid(x):
    return 0.5 * jnp.tanh(0.5 * x) + 0.5


def bulk_wait(ref, sem):
    pltpu.make_async_copy(ref, ref, sem).wait()


def slot_table(rows, sources, counts, key, rank, order, source, keep, last, filled):
    slots, row_tiles = key.shape[0], last.shape[0]
    count = counts[0, 0]

    @pl.loop(0, slots)
    def _(k):
        key[k] = jnp.where(k < count, rows[0, k], row_tiles) * slots + k

    @pl.loop(0, slots)
    def _(k):
        mine = key[k]
        rank[k] = sum((key[other] < mine).astype(jnp.int32) for other in range(slots))

    @pl.loop(0, slots)
    def _(n):
        slot = sum(jnp.where(rank[k] == n, k, 0) for k in range(slots))
        order[n] = slot
        source[n] = sources[0, slot]
        keep[n] = key[slot] // slots

    @pl.loop(0, row_tiles)
    def _(r):
        ahead = sum((key[k] < (r + 1) * slots).astype(jnp.int32) for k in range(slots))
        below = sum((key[k] < r * slots).astype(jnp.int32) for k in range(slots))
        last[r] = jnp.maximum(ahead - 1, 0)
        filled[r] = (ahead > below).astype(jnp.int32)


def kernel(
    times, slabs, refs,
    rows_hbm, sources_hbm, counts_hbm, lists_hbm, features, values_hbm, w_in_hbm, w_rec_hbm, bias,
    out,
    rows, sources, counts, lists, key, rank, order, source, keep, last_slot, filled,
    values, w_in, w_rec, first0, first1, next0, next1, pack,
    arrived00, arrived01, arrived10, arrived11, sums, mixed, inputs, hidden, final, gates,
    small_sem, load_sem, slab_sem, ahead_sem, back_sem,
):
    time, slab = lax.axis_index("tm"), lax.axis_index("slab")
    slots, row_tiles = key.shape[0], last_slot.shape[0]
    tile = first0.shape[1]
    layers, _, width = w_in.shape
    units = width // 4
    halves = 2
    starts = [times * sum(CHUNKS[:n]) for n in range(len(CHUNKS))]
    chunks = list(enumerate(zip(CHUNKS, starts)))
    current = [[first0, first1], [next0, next1]]
    arrived = [[arrived00, arrived01], [arrived10, arrived11]]

    small = [
        pltpu.make_async_copy(a, b, small_sem.at[n])
        for n, (a, b) in enumerate(
            [(lists_hbm, lists), (rows_hbm, rows), (sources_hbm, sources), (counts_hbm, counts)]
        )
    ]
    loads = [
        pltpu.make_async_copy(a, b, load_sem.at[n])
        for n, (a, b) in enumerate(
            [
                (features.at[:, :, pl.ds(0, LANES)], first0),
                (features.at[:, :, pl.ds(LANES, LANES)], first1),
                (values_hbm, values),
                (w_in_hbm, w_in),
                (w_rec_hbm, w_rec),
            ]
        )
    ]
    for load in small + loads:
        load.start()

    barrier = pltpu.get_barrier_semaphore()

    @pl.loop(1, slabs)
    def _(step):
        pl.semaphore_signal(barrier, device_id={"slab": lax.rem(slab + step, slabs)})

    @pl.loop(1, times)
    def _(step):
        pl.semaphore_signal(barrier, device_id={"tm": lax.rem(time + step, times)})

    small[0].wait()

    def pack_for(layer, half, q, target):
        for j in range(refs):
            target[j] = current[layer][half][lists[0, q, slab * refs + j]]

    def pack_all(layer, half):
        @pl.loop(1, slabs)
        def _(step):
            q = lax.rem(slab + step, slabs)
            pack_for(layer, half, q, pack.at[layer, half, q])

        pack_for(layer, half, slab, arrived[layer][half].at[pl.ds(slab * refs, refs)])

    def send_slab(layer, half):
        @pl.loop(1, slabs)
        def _(step):
            q = lax.rem(slab + step, slabs)
            pltpu.make_async_remote_copy(
                src_ref=pack.at[layer, half, q],
                dst_ref=arrived[layer][half].at[pl.ds(slab * refs, refs)],
                send_sem=slab_sem.at[layer, half, 0],
                recv_sem=slab_sem.at[layer, half, 1],
                device_id={"slab": q},
            ).start()

    def slab_wait(layer, half, end):
        bulk_wait(pack.at[layer, half, pl.ds(0, slabs - 1)], slab_sem.at[layer, half, end])

    def add_slots(layer, half):
        total = jnp.zeros((tile, LANES), jnp.float32)
        for n in range(slots):
            product = jnp.dot(
                values[order[n]],
                arrived[layer][half][source[n]],
                preferred_element_type=jnp.float32,
            )
            if n > 0:
                same = (keep[n] == keep[n - 1]).astype(jnp.int32).astype(jnp.float32)
                product = total * same + product
            total = product
            sums[n] = total
        for r in range(row_tiles):
            live = filled[r].astype(jnp.float32)
            mixed[layer, half, r * tile : (r + 1) * tile, :] = (sums[last_slot[r]] * live).astype(
                jnp.bfloat16
            )

    def send_ahead(layer, half, n, size, start):
        @pl.loop(1, times)
        def _(step):
            peer = lax.rem(time + step, times)
            pltpu.make_async_remote_copy(
                src_ref=mixed.at[layer, half, pl.ds(start + peer * size, size)],
                dst_ref=inputs.at[layer, half, pl.ds(start + time * size, size)],
                send_sem=ahead_sem.at[layer, half, n, 0],
                recv_sem=ahead_sem.at[layer, half, n, 1],
                device_id={"tm": peer},
            ).start()

        own = pl.ds(pl.multiple_of(start + time * size, size), size)
        inputs[layer, half, own, :] = mixed[layer, half, own, :]

    def project(layer, size, start):
        block = 8 * size

        @pl.loop(0, times // 8)
        def _(m):
            part = pl.ds(pl.multiple_of(start + m * block, block), block)
            both = jnp.concatenate([inputs[layer, half, part, :] for half in range(halves)], axis=1)
            gates[part, :] = (
                jnp.dot(both, w_in[layer], preferred_element_type=jnp.float32)
                + bias[layer : layer + 1, :]
            )

    def recur(layer, size, start):
        def advance(t, state):
            before, memory = state
            part = pl.ds(pl.multiple_of(start + t * size, size), size)
            total = gates[part, :] + jnp.dot(
                before, w_rec[layer], preferred_element_type=jnp.float32
            )
            in_gate, forget, candidate, out_gate = (
                total[:, k * units : (k + 1) * units] for k in range(4)
            )
            memory = sigmoid(forget) * memory + sigmoid(in_gate) * jnp.tanh(candidate)
            after = (sigmoid(out_gate) * jnp.tanh(memory)).astype(jnp.bfloat16)
            if layer == layers - 1:
                final[part, :] = after
            else:
                for half in range(halves):
                    hidden[half, part, :] = after[:, half * LANES : (half + 1) * LANES]
            return after, memory

        lax.fori_loop(
            0, times, advance,
            (jnp.zeros((size, units), jnp.bfloat16), jnp.zeros((size, units), jnp.float32)),
            unroll=4,
        )

    def send_back(source_ref, target_ref, sems, size, start):
        home = (start + time * size) // tile
        place = pl.ds(pl.multiple_of(lax.rem(start + time * size, tile), size), size)

        @pl.loop(1, times)
        def _(step):
            peer = lax.rem(time + step, times)
            pltpu.make_async_remote_copy(
                src_ref=source_ref.at[pl.ds(start + peer * size, size)],
                dst_ref=target_ref.at[home, place],
                send_sem=sems.at[0],
                recv_sem=sems.at[1],
                device_id={"tm": peer},
            ).start()

        own = pl.ds(pl.multiple_of(start + time * size, size), size)
        target_ref[home, place, :] = source_ref[own, :]

    most = [pl.ds(start, (times - 1) * size) for _, (size, start) in chunks]

    loads[0].wait()
    pack_all(0, 0)
    pl.semaphore_wait(barrier, slabs - 1 + times - 1)

    for layer in range(layers):
        send_slab(layer, 0)
        if layer == 0:
            loads[1].wait()
        else:
            for n, _ in chunks:
                bulk_wait(hidden.at[1, most[n]], back_sem.at[layer - 1, 1, n, 1])
        pack_all(layer, 1)
        slab_wait(layer, 0, 0)
        send_slab(layer, 1)
        if layer == 0:
            for load in small[1:]:
                load.wait()
            slot_table(
                rows, sources, counts, key, rank, order, source, keep, last_slot, filled
            )
            loads[2].wait()

        for half in range(halves):
            slab_wait(layer, half, 1)
            add_slots(layer, half)
            for n, (size, start) in chunks:
                send_ahead(layer, half, n, size, start)

        if layer == 0:
            loads[3].wait()
            loads[4].wait()

        for n, (size, start) in chunks:
            for half in range(halves):
                bulk_wait(inputs.at[layer, half, most[n]], ahead_sem.at[layer, half, n, 1])
            project(layer, size, start)
            recur(layer, size, start)
            if layer == layers - 1:
                send_back(final, out, back_sem.at[layer, 0, n], size, start)
            else:
                for half in range(halves):
                    send_back(
                        hidden.at[half], current[layer + 1][half], back_sem.at[layer, half, n], size, start
                    )

        if layer == layers - 1:
            for n, _ in chunks:
                bulk_wait(final.at[most[n]], back_sem.at[layer, 0, n, 1])
        else:
            for n, _ in chunks:
                bulk_wait(hidden.at[0, most[n]], back_sem.at[layer, 0, n, 1])
            pack_all(layer + 1, 0)

    for layer in range(layers):
        slab_wait(layer, 1, 0)
        for n, _ in chunks:
            for half in range(halves):
                bulk_wait(mixed.at[layer, half, most[n]], ahead_sem.at[layer, half, n, 0])
            if layer == layers - 1:
                bulk_wait(final.at[most[n]], back_sem.at[layer, 0, n, 0])
            else:
                for half in range(halves):
                    bulk_wait(hidden.at[half, most[n]], back_sem.at[layer, half, n, 0])


def local(
    features, ref_lists, tile_rows, tile_sources, tile_counts, tile_values, w_input, w_hidden, bias
):
    _, rows, width = features.shape
    _, slots, tile, _ = tile_values.shape
    layers, units = w_hidden.shape[:2]
    slabs, times = lax.axis_size("slab"), lax.axis_size("tm")
    refs = ref_lists.shape[2] // slabs
    row_tiles, listed, halves, parts = rows // tile, slabs * refs, width // LANES, len(CHUNKS)
    vmem = pl.BlockSpec(memory_space=pltpu.VMEM)
    anywhere = pl.BlockSpec(memory_space=pl.ANY)
    narrow = pltpu.VMEM((row_tiles, tile, LANES), jnp.bfloat16)
    landing = pltpu.VMEM((listed, tile, LANES), jnp.bfloat16)
    half_rows = pltpu.VMEM((layers, halves, rows, LANES), jnp.bfloat16)
    result = pl.pallas_call(
        functools.partial(kernel, times, slabs, refs),
        out_shape=jax.ShapeDtypeStruct((row_tiles, tile, units), jnp.bfloat16),
        in_specs=[anywhere] * 8 + [vmem],
        out_specs=vmem,
        scratch_shapes=[
            pltpu.SMEM(tile_rows.shape, jnp.int32),
            pltpu.SMEM(tile_sources.shape, jnp.int32),
            pltpu.SMEM(tile_counts.shape, jnp.int32),
            pltpu.SMEM(ref_lists.shape, jnp.int32),
            *[pltpu.SMEM((slots,), jnp.int32)] * 5,
            *[pltpu.SMEM((row_tiles,), jnp.int32)] * 2,
            pltpu.VMEM(tile_values.shape[1:], jnp.bfloat16),
            pltpu.VMEM(w_input.shape, jnp.bfloat16),
            pltpu.VMEM(w_hidden.shape, jnp.bfloat16),
            *[narrow] * 4,
            pltpu.VMEM((layers, halves, slabs, refs, tile, LANES), jnp.bfloat16),
            *[landing] * 4,
            pltpu.VMEM((slots, tile, LANES), jnp.float32),
            half_rows,
            half_rows,
            pltpu.VMEM((halves, rows, LANES), jnp.bfloat16),
            pltpu.VMEM((rows, units), jnp.bfloat16),
            pltpu.VMEM((rows, 4 * units), jnp.float32),
            pltpu.SemaphoreType.DMA((4,)),
            pltpu.SemaphoreType.DMA((5,)),
            pltpu.SemaphoreType.DMA((layers, halves, 2)),
            pltpu.SemaphoreType.DMA((layers, halves, parts, 2)),
            pltpu.SemaphoreType.DMA((layers, halves, parts, 2)),
        ],
        compiler_params=pltpu.CompilerParams(
            collective_id=0, has_side_effects=True, vmem_limit_bytes=56 << 20
        ),
    )(
        tile_rows, tile_sources, tile_counts, ref_lists,
        features[0].reshape(row_tiles, tile, width), tile_values[0], w_input, w_hidden, bias,
    )
    return result.reshape(1, rows, units)


def solution(mesh):
    in_specs = (
        P("tm", "slab", None),
        P("tm", None, None),
        P("tm", "slab"),
        P("tm", "slab"),
        P("tm", "slab"),
        P("tm", "slab", None, None),
        P(),
        P(),
        P(),
    )
    out_specs = P("tm", "slab", None)
    return jax.shard_map(local, mesh=mesh, in_specs=in_specs, out_specs=out_specs, check_vma=False)
```

```python
import functools

import jax
import jax.numpy as jnp
from jax import lax
from jax.experimental import pallas as pl
from jax.experimental.pallas import tpu as pltpu
from jax.sharding import PartitionSpec as P

CHUNKS = ((16, 32), (16, 32))
BURST = 4
SMALL = 16
LANES = 128


def sigmoid(x):
    return 0.5 * jnp.tanh(0.5 * x) + 0.5


def bulk_wait(ref, sem):
    pltpu.make_async_copy(ref, ref, sem).wait()


def slot_table(rows, sources, counts, key, rank, order, source, keep, last, filled):
    slots, row_tiles = key.shape[0], last.shape[0]
    count = counts[0, 0]

    @pl.loop(0, slots)
    def _(k):
        key[k] = jnp.where(k < count, rows[0, k], row_tiles) * slots + k

    @pl.loop(0, slots)
    def _(k):
        mine = key[k]
        rank[k] = sum((key[other] < mine).astype(jnp.int32) for other in range(slots))

    @pl.loop(0, slots)
    def _(n):
        slot = sum(jnp.where(rank[k] == n, k, 0) for k in range(slots))
        order[n] = slot
        source[n] = sources[0, slot]
        keep[n] = key[slot] // slots

    @pl.loop(0, row_tiles)
    def _(r):
        ahead = sum((key[k] < (r + 1) * slots).astype(jnp.int32) for k in range(slots))
        below = sum((key[k] < r * slots).astype(jnp.int32) for k in range(slots))
        last[r] = jnp.maximum(ahead - 1, 0)
        filled[r] = (ahead > below).astype(jnp.int32)


def kernel(
    times, slabs, refs,
    rows_hbm, sources_hbm, counts_hbm, lists_hbm, features, values_hbm, w_in_hbm, w_rec_hbm, bias_hbm,
    out,
    rows, sources, counts, lists, key, rank, order, source, keep, last_slot, filled,
    values, w_in, w_rec, bias, first0, first1, next0, next1, pack,
    arrived00, arrived01, arrived10, arrived11, sums, mixed, inputs, hidden, final, gates,
    small_sem, load_sem, slab_sem, ahead_sem, back_sem,
):
    time, slab = lax.axis_index("tm"), lax.axis_index("slab")
    slots, row_tiles = key.shape[0], last_slot.shape[0]
    tile = first0.shape[1]
    layers, _, width = w_in.shape
    units = width // 4
    halves = 2
    parts = [len(sizes) for sizes in CHUNKS]
    starts = [[times * sum(sizes[:n]) for n in range(len(sizes))] for sizes in CHUNKS]
    current = [[first0, first1], [next0, next1]]
    arrived = [[arrived00, arrived01], [arrived10, arrived11]]

    small = [
        pltpu.make_async_copy(a, b, small_sem.at[n])
        for n, (a, b) in enumerate(
            [(lists_hbm, lists), (rows_hbm, rows), (sources_hbm, sources), (counts_hbm, counts)]
        )
    ]
    loads = [
        pltpu.make_async_copy(a, b, load_sem.at[n])
        for n, (a, b) in enumerate(
            [
                (features.at[:, :, pl.ds(0, LANES)], first0),
                (features.at[:, :, pl.ds(LANES, LANES)], first1),
                (values_hbm, values),
                (w_in_hbm, w_in),
                (w_rec_hbm, w_rec),
                (bias_hbm, bias),
            ]
        )
    ]
    for load in small + loads:
        load.start()

    barrier = pltpu.get_barrier_semaphore()

    @pl.loop(1, slabs)
    def _(step):
        pl.semaphore_signal(barrier, device_id={"slab": lax.rem(slab + step, slabs)})

    @pl.loop(1, times)
    def _(step):
        pl.semaphore_signal(barrier, device_id={"tm": lax.rem(time + step, times)})

    small[0].wait()

    def pack_for(layer, half, q, target):
        for j in range(refs):
            target[j] = current[layer][half][lists[0, q, slab * refs + j]]

    def pack_all(layer, half):
        @pl.loop(1, slabs)
        def _(step):
            q = lax.rem(slab + step, slabs)
            pack_for(layer, half, q, pack.at[layer, half, q])

        pack_for(layer, half, slab, arrived[layer][half].at[pl.ds(slab * refs, refs)])

    def send_slab(layer, half):
        for step in range(1, slabs):
            q = lax.rem(slab + step, slabs)
            pltpu.make_async_remote_copy(
                src_ref=pack.at[layer, half, q],
                dst_ref=arrived[layer][half].at[pl.ds(slab * refs, refs)],
                send_sem=slab_sem.at[layer, half, 0],
                recv_sem=slab_sem.at[layer, half, 1],
                device_id={"slab": q},
            ).start()

    def slab_wait(layer, half, end):
        bulk_wait(pack.at[layer, half, pl.ds(0, slabs - 1)], slab_sem.at[layer, half, end])

    def add_slots(layer, half):
        total = jnp.zeros((tile, LANES), jnp.float32)
        for n in range(slots):
            product = jnp.dot(
                values[order[n]],
                arrived[layer][half][source[n]],
                preferred_element_type=jnp.float32,
            )
            if n > 0:
                same = (keep[n] == keep[n - 1]).astype(jnp.int32).astype(jnp.float32)
                product = total * same + product
            total = product
            sums[n] = total
        for r in range(row_tiles):
            live = filled[r].astype(jnp.float32)
            mixed[layer, half, r * tile : (r + 1) * tile, :] = (sums[last_slot[r]] * live).astype(
                jnp.bfloat16
            )

    def rows_of(layer, n, device):
        size, start = CHUNKS[layer][n], starts[layer][n]
        return pl.ds(pl.multiple_of(start + device * size, size), size)

    def every_peer(send):
        @pl.loop(1, times)
        def _(step):
            send(lax.rem(time + step, times))

    def send_ahead(layer, half, n):
        def send(peer):
            pltpu.make_async_remote_copy(
                src_ref=mixed.at[layer, half, rows_of(layer, n, peer)],
                dst_ref=inputs.at[layer, half, rows_of(layer, n, time)],
                send_sem=ahead_sem.at[layer, half, n, 0],
                recv_sem=ahead_sem.at[layer, half, n, 1],
                device_id={"tm": peer},
            ).start()

        return send

    def keep_own(layer, half, n):
        inputs[layer, half, rows_of(layer, n, time), :] = mixed[layer, half, rows_of(layer, n, time), :]

    def projected(layer, part):
        both = jnp.concatenate([inputs[layer, half, part, :] for half in range(halves)], axis=1)
        return (
            jnp.dot(both, w_in[layer], preferred_element_type=jnp.float32)
            + bias[layer : layer + 1, :]
        )

    def project(layer, n):
        size, start = CHUNKS[layer][n], starts[layer][n]
        block = 8 * size

        @pl.loop(0, times // 8)
        def _(m):
            part = pl.ds(pl.multiple_of(start + m * block, block), block)
            gates[part, :] = projected(layer, part)

    def recur(layer, n, send=None):
        size = CHUNKS[layer][n]

        def advance(t, state):
            before, memory = state
            part = rows_of(layer, n, t)
            total = projected(layer, part) if size <= SMALL else gates[part, :]
            total = total + jnp.dot(before, w_rec[layer], preferred_element_type=jnp.float32)
            in_gate, forget, candidate, out_gate = (
                total[:, k * units : (k + 1) * units] for k in range(4)
            )
            memory = sigmoid(forget) * memory + sigmoid(in_gate) * jnp.tanh(candidate)
            after = (sigmoid(out_gate) * jnp.tanh(memory)).astype(jnp.bfloat16)
            if layer == layers - 1:
                final[part, :] = after
            else:
                for half in range(halves):
                    hidden[half, part, :] = after[:, half * LANES : (half + 1) * LANES]
            return after, memory

        zero = (jnp.zeros((size, units), jnp.bfloat16), jnp.zeros((size, units), jnp.float32))
        if send is None:
            lax.fori_loop(0, times, advance, zero, unroll=8)
            return

        def burst(m, state):
            for k in range(BURST):
                state = advance(m * BURST + k, state)
            for k in range(1, BURST):
                send(m * BURST + lax.rem(time + k, BURST))

            @pl.when(m != time // BURST)
            def _():
                send(m * BURST + lax.rem(time, BURST))

            return state

        lax.fori_loop(0, times // BURST, burst, zero)

    def returned(layer, half):
        if layer == layers - 1:
            return final, out
        return hidden.at[half], current[layer + 1][half]

    def send_back(layer, half, n):
        kept, target = returned(layer, half)
        row = starts[layer][n] + time * CHUNKS[layer][n]
        place = pl.ds(pl.multiple_of(lax.rem(row, tile), CHUNKS[layer][n]), CHUNKS[layer][n])

        def send(peer):
            pltpu.make_async_remote_copy(
                src_ref=kept.at[rows_of(layer, n, peer)],
                dst_ref=target.at[row // tile, place],
                send_sem=back_sem.at[layer, half, n, 0],
                recv_sem=back_sem.at[layer, half, n, 1],
                device_id={"tm": peer},
            ).start()

        return send

    def return_own(layer, half, n):
        kept, target = returned(layer, half)
        row = starts[layer][n] + time * CHUNKS[layer][n]
        place = pl.ds(pl.multiple_of(lax.rem(row, tile), CHUNKS[layer][n]), CHUNKS[layer][n])
        target[row // tile, place, :] = kept[rows_of(layer, n, time), :]

    def peers_bytes(layer, n):
        return pl.ds(starts[layer][n], (times - 1) * CHUNKS[layer][n])

    loads[0].wait()
    pack_all(0, 0)
    pl.semaphore_wait(barrier, slabs - 1 + times - 1)

    for layer in range(layers):
        back_halves = range(1 if layer == layers - 1 else halves)
        final_part = parts[layer] - 1
        send_slab(layer, 0)
        if layer == 0:
            loads[1].wait()
        else:
            for n in range(parts[layer - 1]):
                bulk_wait(hidden.at[1, peers_bytes(layer - 1, n)], back_sem.at[layer - 1, 1, n, 1])
        pack_all(layer, 1)
        send_slab(layer, 1)
        if layer == 0:
            for load in small[1:]:
                load.wait()
            slot_table(
                rows, sources, counts, key, rank, order, source, keep, last_slot, filled
            )
            for load in loads[2:]:
                load.wait()

        for half in range(halves):
            slab_wait(layer, half, 1)
            add_slots(layer, half)
            for n in range(parts[layer]):
                every_peer(send_ahead(layer, half, n))
                keep_own(layer, half, n)

        for n in range(parts[layer]):
            for half in range(halves):
                bulk_wait(inputs.at[layer, half, peers_bytes(layer, n)], ahead_sem.at[layer, half, n, 1])
            if CHUNKS[layer][n] > SMALL:
                project(layer, n)
            if n < final_part:
                recur(layer, n)
                for half in back_halves:
                    every_peer(send_back(layer, half, n))
            else:
                recur(layer, n, send_back(layer, 0, n))
            for half in back_halves:
                return_own(layer, half, n)

        if layer == layers - 1:
            for n in range(parts[layer]):
                bulk_wait(final.at[peers_bytes(layer, n)], back_sem.at[layer, 0, n, 1])
        else:
            bulk_wait(hidden.at[0, peers_bytes(layer, final_part)], back_sem.at[layer, 0, final_part, 0])
            every_peer(send_back(layer, 1, final_part))
            for n in range(parts[layer]):
                bulk_wait(hidden.at[0, peers_bytes(layer, n)], back_sem.at[layer, 0, n, 1])
            pack_all(layer + 1, 0)

    for layer in range(layers):
        for half in range(halves):
            slab_wait(layer, half, 0)
        for n in range(parts[layer]):
            for half in range(halves):
                bulk_wait(mixed.at[layer, half, peers_bytes(layer, n)], ahead_sem.at[layer, half, n, 0])
            if layer == layers - 1:
                bulk_wait(final.at[peers_bytes(layer, n)], back_sem.at[layer, 0, n, 0])
            else:
                for half in range(halves):
                    if n < parts[layer] - 1 or half > 0:
                        bulk_wait(hidden.at[half, peers_bytes(layer, n)], back_sem.at[layer, half, n, 0])


def local(
    features, ref_lists, tile_rows, tile_sources, tile_counts, tile_values, w_input, w_hidden, bias
):
    _, rows, width = features.shape
    _, slots, tile, _ = tile_values.shape
    layers, units = w_hidden.shape[:2]
    slabs, times = lax.axis_size("slab"), lax.axis_size("tm")
    refs = ref_lists.shape[2] // slabs
    row_tiles, listed, halves = rows // tile, slabs * refs, width // LANES
    parts = max(len(sizes) for sizes in CHUNKS)
    vmem = pl.BlockSpec(memory_space=pltpu.VMEM)
    far = pl.BlockSpec(memory_space=pltpu.HBM)
    narrow = pltpu.VMEM((row_tiles, tile, LANES), jnp.bfloat16)
    landing = pltpu.VMEM((listed, tile, LANES), jnp.bfloat16)
    half_rows = pltpu.VMEM((layers, halves, rows, LANES), jnp.bfloat16)
    result = pl.pallas_call(
        functools.partial(kernel, times, slabs, refs),
        out_shape=jax.ShapeDtypeStruct((row_tiles, tile, units), jnp.bfloat16),
        in_specs=[far] * 9,
        out_specs=vmem,
        scratch_shapes=[
            pltpu.SMEM(tile_rows.shape, jnp.int32),
            pltpu.SMEM(tile_sources.shape, jnp.int32),
            pltpu.SMEM(tile_counts.shape, jnp.int32),
            pltpu.SMEM(ref_lists.shape, jnp.int32),
            *[pltpu.SMEM((slots,), jnp.int32)] * 5,
            *[pltpu.SMEM((row_tiles,), jnp.int32)] * 2,
            pltpu.VMEM(tile_values.shape[1:], jnp.bfloat16),
            pltpu.VMEM(w_input.shape, jnp.bfloat16),
            pltpu.VMEM(w_hidden.shape, jnp.bfloat16),
            pltpu.VMEM(bias.shape, jnp.float32),
            *[narrow] * 4,
            pltpu.VMEM((layers, halves, slabs, refs, tile, LANES), jnp.bfloat16),
            *[landing] * 4,
            pltpu.VMEM((slots, tile, LANES), jnp.float32),
            half_rows,
            half_rows,
            pltpu.VMEM((halves, rows, LANES), jnp.bfloat16),
            pltpu.VMEM((rows, units), jnp.bfloat16),
            pltpu.VMEM((rows, 4 * units), jnp.float32),
            pltpu.SemaphoreType.DMA((4,)),
            pltpu.SemaphoreType.DMA((6,)),
            pltpu.SemaphoreType.DMA((layers, halves, 2)),
            pltpu.SemaphoreType.DMA((layers, halves, parts, 2)),
            pltpu.SemaphoreType.DMA((layers, halves, parts, 2)),
        ],
        compiler_params=pltpu.CompilerParams(
            collective_id=0, has_side_effects=True, vmem_limit_bytes=52 << 20
        ),
    )(
        tile_rows, tile_sources, tile_counts, ref_lists,
        features[0].reshape(row_tiles, tile, width), tile_values[0], w_input, w_hidden, bias,
    )
    return result.reshape(1, rows, units)


def solution(mesh):
    in_specs = (
        P("tm", "slab", None),
        P("tm", None, None),
        P("tm", "slab"),
        P("tm", "slab"),
        P("tm", "slab"),
        P("tm", "slab", None, None),
        P(),
        P(),
        P(),
    )
    out_specs = P("tm", "slab", None)
    return jax.shard_map(local, mesh=mesh, in_specs=in_specs, out_specs=out_specs, check_vma=False)
```

```python
import functools

import jax
import jax.numpy as jnp
from jax import lax
from jax.experimental import pallas as pl
from jax.experimental.pallas import tpu as pltpu
from jax.sharding import PartitionSpec as P

CHUNKS = ((16, 32), (16, 32))
BURST = 4
SMALL = 16
UNROLL = 8
LANES = 128


def sigmoid(x):
    return 0.5 * jnp.tanh(0.5 * x) + 0.5


def bulk_wait(ref, sem):
    pltpu.make_async_copy(ref, ref, sem).wait()


def slot_table(rows, sources, counts, key, rank, order, source, keep, last, filled):
    slots, row_tiles = key.shape[0], last.shape[0]
    count = counts[0, 0]

    @pl.loop(0, slots)
    def _(k):
        key[k] = jnp.where(k < count, rows[0, k], row_tiles) * slots + k

    @pl.loop(0, slots)
    def _(k):
        mine = key[k]
        rank[k] = sum((key[other] < mine).astype(jnp.int32) for other in range(slots))

    @pl.loop(0, slots)
    def _(n):
        slot = sum(jnp.where(rank[k] == n, k, 0) for k in range(slots))
        order[n] = slot
        source[n] = sources[0, slot]
        keep[n] = key[slot] // slots

    @pl.loop(0, row_tiles)
    def _(r):
        ahead = sum((key[k] < (r + 1) * slots).astype(jnp.int32) for k in range(slots))
        below = sum((key[k] < r * slots).astype(jnp.int32) for k in range(slots))
        last[r] = jnp.maximum(ahead - 1, 0)
        filled[r] = (ahead > below).astype(jnp.int32)


def kernel(
    times, slabs, refs,
    rows_hbm, sources_hbm, counts_hbm, lists_hbm, features, values_hbm, w_in_hbm, w_rec_hbm, bias_hbm,
    out,
    rows, sources, counts, lists, key, rank, order, source, keep, last_slot, filled,
    values, w_in, w_rec, bias, first0, first1, next0, next1, pack,
    arrived00, arrived01, arrived10, arrived11, sums, mixed, inputs, hidden, final, gates_even, gates_odd,
    small_sem, load_sem, slab_sem, ahead_sem, back_sem,
):
    time, slab = lax.axis_index("tm"), lax.axis_index("slab")
    slots, row_tiles = key.shape[0], last_slot.shape[0]
    tile = first0.shape[1]
    layers, _, width = w_in.shape
    units = width // 4
    halves = 2
    parts = [len(sizes) for sizes in CHUNKS]
    starts = [[times * sum(sizes[:n]) for n in range(len(sizes))] for sizes in CHUNKS]
    current = [[first0, first1], [next0, next1]]
    arrived = [[arrived00, arrived01], [arrived10, arrived11]]

    small = [
        pltpu.make_async_copy(a, b, small_sem.at[n])
        for n, (a, b) in enumerate(
            [(lists_hbm, lists), (rows_hbm, rows), (sources_hbm, sources), (counts_hbm, counts)]
        )
    ]
    loads = [
        pltpu.make_async_copy(a, b, load_sem.at[n])
        for n, (a, b) in enumerate(
            [
                (features.at[:, :, pl.ds(0, LANES)], first0),
                (features.at[:, :, pl.ds(LANES, LANES)], first1),
                (values_hbm, values),
                (w_in_hbm, w_in),
                (w_rec_hbm, w_rec),
                (bias_hbm, bias),
            ]
        )
    ]
    for load in small + loads:
        load.start()

    barrier = pltpu.get_barrier_semaphore()

    @pl.loop(1, slabs)
    def _(step):
        pl.semaphore_signal(barrier, device_id={"slab": lax.rem(slab + step, slabs)})

    @pl.loop(1, times)
    def _(step):
        pl.semaphore_signal(barrier, device_id={"tm": lax.rem(time + step, times)})

    small[0].wait()

    def pack_for(layer, half, q, target):
        for j in range(refs):
            target[j] = current[layer][half][lists[0, q, slab * refs + j]]

    def pack_all(layer, half):
        @pl.loop(1, slabs)
        def _(step):
            q = lax.rem(slab + step, slabs)
            pack_for(layer, half, q, pack.at[layer, half, q])

        pack_for(layer, half, slab, arrived[layer][half].at[pl.ds(slab * refs, refs)])

    def send_slab(layer, half):
        for step in range(1, slabs):
            q = lax.rem(slab + step, slabs)
            pltpu.make_async_remote_copy(
                src_ref=pack.at[layer, half, q],
                dst_ref=arrived[layer][half].at[pl.ds(slab * refs, refs)],
                send_sem=slab_sem.at[layer, half, 0],
                recv_sem=slab_sem.at[layer, half, 1],
                device_id={"slab": q},
            ).start()

    def slab_wait(layer, half, end):
        bulk_wait(pack.at[layer, half, pl.ds(0, slabs - 1)], slab_sem.at[layer, half, end])

    def add_slots(layer, half):
        total = jnp.zeros((tile, LANES), jnp.float32)
        for n in range(slots):
            product = jnp.dot(
                values[order[n]],
                arrived[layer][half][source[n]],
                preferred_element_type=jnp.float32,
            )
            if n > 0:
                same = (keep[n] == keep[n - 1]).astype(jnp.int32).astype(jnp.float32)
                product = total * same + product
            total = product
            sums[n] = total
        for r in range(row_tiles):
            live = filled[r].astype(jnp.float32)
            mixed[layer, half, r * tile : (r + 1) * tile, :] = (sums[last_slot[r]] * live).astype(
                jnp.bfloat16
            )

    def rows_of(layer, n, device):
        size, start = CHUNKS[layer][n], starts[layer][n]
        return pl.ds(pl.multiple_of(start + device * size, size), size)

    def every_peer(send):
        @pl.loop(1, times)
        def _(step):
            send(lax.rem(time + step, times))

    def send_ahead(layer, half, n):
        def send(peer):
            pltpu.make_async_remote_copy(
                src_ref=mixed.at[layer, half, rows_of(layer, n, peer)],
                dst_ref=inputs.at[layer, half, rows_of(layer, n, time)],
                send_sem=ahead_sem.at[layer, half, n, 0],
                recv_sem=ahead_sem.at[layer, half, n, 1],
                device_id={"tm": peer},
            ).start()

        return send

    def keep_own(layer, half, n):
        inputs[layer, half, rows_of(layer, n, time), :] = mixed[layer, half, rows_of(layer, n, time), :]

    def projected(layer, part):
        both = jnp.concatenate([inputs[layer, half, part, :] for half in range(halves)], axis=1)
        return (
            jnp.dot(both, w_in[layer], preferred_element_type=jnp.float32)
            + bias[layer : layer + 1, :]
        )

    def recur(layer, n, send=None):
        size = CHUNKS[layer][n]

        def advance(t, state, gate_inputs):
            before, memory = state
            part = rows_of(layer, n, t)
            total = gate_inputs + jnp.dot(
                before, w_rec[layer], preferred_element_type=jnp.float32
            )
            in_gate, forget, candidate, out_gate = (
                total[:, k * units : (k + 1) * units] for k in range(4)
            )
            memory = sigmoid(forget) * memory + sigmoid(in_gate) * jnp.tanh(candidate)
            after = (sigmoid(out_gate) * jnp.tanh(memory)).astype(jnp.bfloat16)
            if layer == layers - 1:
                final[part, :] = after
            else:
                for half in range(halves):
                    hidden[half, part, :] = after[:, half * LANES : (half + 1) * LANES]
            return after, memory

        def step(t, state):
            return advance(t, state, projected(layer, rows_of(layer, n, t)))

        zero = (jnp.zeros((size, units), jnp.bfloat16), jnp.zeros((size, units), jnp.float32))
        if size <= SMALL and send is None:
            lax.fori_loop(0, times, step, zero, unroll=UNROLL)
            return

        bursts = times // BURST
        block = BURST * size

        def project(m, target):
            start = starts[layer][n] + jnp.minimum(m, bursts - 1) * block
            target[0:block, :] = projected(layer, pl.ds(pl.multiple_of(start, block), block))

        def burst(m, state, ready):
            for k in range(BURST):
                if size <= SMALL:
                    state = step(m * BURST + k, state)
                else:
                    state = advance(m * BURST + k, state, ready[k * size : (k + 1) * size, :])
            if send is not None:
                for k in range(1, BURST):
                    send(m * BURST + lax.rem(time + k, BURST))

                @pl.when(m != time // BURST)
                def _():
                    send(m * BURST + lax.rem(time, BURST))

            return state

        def two_bursts(m, state):
            for at, (ready, coming) in enumerate([(gates_even, gates_odd), (gates_odd, gates_even)]):
                if size > SMALL:
                    project(2 * m + at + 1, coming)
                state = burst(2 * m + at, state, ready)
            return state

        if size > SMALL:
            project(jnp.int32(0), gates_even)
        lax.fori_loop(0, bursts // 2, two_bursts, zero)

    def returned(layer, half):
        if layer == layers - 1:
            return final, out
        return hidden.at[half], current[layer + 1][half]

    def send_back(layer, half, n):
        kept, target = returned(layer, half)
        row = starts[layer][n] + time * CHUNKS[layer][n]
        place = pl.ds(pl.multiple_of(lax.rem(row, tile), CHUNKS[layer][n]), CHUNKS[layer][n])

        def send(peer):
            pltpu.make_async_remote_copy(
                src_ref=kept.at[rows_of(layer, n, peer)],
                dst_ref=target.at[row // tile, place],
                send_sem=back_sem.at[layer, half, n, 0],
                recv_sem=back_sem.at[layer, half, n, 1],
                device_id={"tm": peer},
            ).start()

        return send

    def return_own(layer, half, n):
        kept, target = returned(layer, half)
        row = starts[layer][n] + time * CHUNKS[layer][n]
        place = pl.ds(pl.multiple_of(lax.rem(row, tile), CHUNKS[layer][n]), CHUNKS[layer][n])
        target[row // tile, place, :] = kept[rows_of(layer, n, time), :]

    def peers_bytes(layer, n):
        return pl.ds(starts[layer][n], (times - 1) * CHUNKS[layer][n])

    loads[0].wait()
    pack_all(0, 0)
    pl.semaphore_wait(barrier, slabs - 1 + times - 1)

    for layer in range(layers):
        back_halves = range(1 if layer == layers - 1 else halves)
        final_part = parts[layer] - 1
        send_slab(layer, 0)
        if layer == 0:
            loads[1].wait()
        else:
            for n in range(parts[layer - 1]):
                bulk_wait(hidden.at[1, peers_bytes(layer - 1, n)], back_sem.at[layer - 1, 1, n, 1])
        pack_all(layer, 1)
        send_slab(layer, 1)
        if layer == 0:
            for load in small[1:]:
                load.wait()
            slot_table(
                rows, sources, counts, key, rank, order, source, keep, last_slot, filled
            )
            for load in loads[2:]:
                load.wait()

        for half in range(halves):
            slab_wait(layer, half, 1)
            add_slots(layer, half)
            for n in range(parts[layer]):
                every_peer(send_ahead(layer, half, n))
                keep_own(layer, half, n)

        for n in range(parts[layer]):
            for half in range(halves):
                bulk_wait(inputs.at[layer, half, peers_bytes(layer, n)], ahead_sem.at[layer, half, n, 1])
            if n < final_part:
                recur(layer, n)
                for half in back_halves:
                    every_peer(send_back(layer, half, n))
            else:
                recur(layer, n, send_back(layer, 0, n))
            for half in back_halves:
                return_own(layer, half, n)

        if layer == layers - 1:
            for n in range(parts[layer]):
                bulk_wait(final.at[peers_bytes(layer, n)], back_sem.at[layer, 0, n, 1])
        else:
            bulk_wait(hidden.at[0, peers_bytes(layer, final_part)], back_sem.at[layer, 0, final_part, 0])
            every_peer(send_back(layer, 1, final_part))
            for n in range(parts[layer]):
                bulk_wait(hidden.at[0, peers_bytes(layer, n)], back_sem.at[layer, 0, n, 1])
            pack_all(layer + 1, 0)

    for layer in range(layers):
        for half in range(halves):
            slab_wait(layer, half, 0)
        for n in range(parts[layer]):
            for half in range(halves):
                bulk_wait(mixed.at[layer, half, peers_bytes(layer, n)], ahead_sem.at[layer, half, n, 0])
            if layer == layers - 1:
                bulk_wait(final.at[peers_bytes(layer, n)], back_sem.at[layer, 0, n, 0])
            else:
                for half in range(halves):
                    if n < parts[layer] - 1 or half > 0:
                        bulk_wait(hidden.at[half, peers_bytes(layer, n)], back_sem.at[layer, half, n, 0])


def pinned(x):
    return pltpu.with_memory_space_constraint(x, pltpu.HBM)


def local(
    features, ref_lists, tile_rows, tile_sources, tile_counts, tile_values, w_input, w_hidden, bias
):
    _, rows, width = features.shape
    _, slots, tile, _ = tile_values.shape
    layers, units = w_hidden.shape[:2]
    slabs, times = lax.axis_size("slab"), lax.axis_size("tm")
    refs = ref_lists.shape[2] // slabs
    row_tiles, listed, halves = rows // tile, slabs * refs, width // LANES
    parts = max(len(sizes) for sizes in CHUNKS)
    vmem = pl.BlockSpec(memory_space=pltpu.VMEM)
    far = pl.BlockSpec(memory_space=pltpu.HBM)
    narrow = pltpu.VMEM((row_tiles, tile, LANES), jnp.bfloat16)
    landing = pltpu.VMEM((listed, tile, LANES), jnp.bfloat16)
    half_rows = pltpu.VMEM((layers, halves, rows, LANES), jnp.bfloat16)
    result = pl.pallas_call(
        functools.partial(kernel, times, slabs, refs),
        out_shape=jax.ShapeDtypeStruct((row_tiles, tile, units), jnp.bfloat16),
        in_specs=[far] * 9,
        out_specs=vmem,
        scratch_shapes=[
            pltpu.SMEM(tile_rows.shape, jnp.int32),
            pltpu.SMEM(tile_sources.shape, jnp.int32),
            pltpu.SMEM(tile_counts.shape, jnp.int32),
            pltpu.SMEM(ref_lists.shape, jnp.int32),
            *[pltpu.SMEM((slots,), jnp.int32)] * 5,
            *[pltpu.SMEM((row_tiles,), jnp.int32)] * 2,
            pltpu.VMEM(tile_values.shape[1:], jnp.bfloat16),
            pltpu.VMEM(w_input.shape, jnp.bfloat16),
            pltpu.VMEM(w_hidden.shape, jnp.bfloat16),
            pltpu.VMEM(bias.shape, jnp.float32),
            *[narrow] * 4,
            pltpu.VMEM((layers, halves, slabs, refs, tile, LANES), jnp.bfloat16),
            *[landing] * 4,
            pltpu.VMEM((slots, tile, LANES), jnp.float32),
            half_rows,
            half_rows,
            pltpu.VMEM((halves, rows, LANES), jnp.bfloat16),
            pltpu.VMEM((rows, units), jnp.bfloat16),
            *[pltpu.VMEM((BURST * max(map(max, CHUNKS)), 4 * units), jnp.float32)] * 2,
            pltpu.SemaphoreType.DMA((4,)),
            pltpu.SemaphoreType.DMA((6,)),
            pltpu.SemaphoreType.DMA((layers, halves, 2)),
            pltpu.SemaphoreType.DMA((layers, halves, parts, 2)),
            pltpu.SemaphoreType.DMA((layers, halves, parts, 2)),
        ],
        compiler_params=pltpu.CompilerParams(
            collective_id=0, has_side_effects=True, vmem_limit_bytes=48 << 20
        ),
    )(
        *map(pinned, (tile_rows, tile_sources)),
        tile_counts,
        *map(pinned, (ref_lists, features[0].reshape(row_tiles, tile, width), tile_values[0])),
        *map(pinned, (w_input, w_hidden, bias)),
    )
    return result.reshape(1, rows, units)


def solution(mesh):
    in_specs = (
        P("tm", "slab", None),
        P("tm", None, None),
        P("tm", "slab"),
        P("tm", "slab"),
        P("tm", "slab"),
        P("tm", "slab", None, None),
        P(),
        P(),
        P(),
    )
    out_specs = P("tm", "slab", None)
    return jax.shard_map(local, mesh=mesh, in_specs=in_specs, out_specs=out_specs, check_vma=False)
```

```python
import functools

import jax
import jax.numpy as jnp
from jax import lax
from jax.experimental import pallas as pl
from jax.experimental.pallas import tpu as pltpu
from jax.sharding import PartitionSpec as P

CHUNKS = ((16, 32), (16, 32))
BURST = 4
SMALL = 16
UNROLL = 8
LANES = 128


def sigmoid(x):
    return 0.5 * jnp.tanh(0.5 * x) + 0.5


def bulk_wait(ref, sem):
    pltpu.make_async_copy(ref, ref, sem).wait()


def slot_table(rows, sources, counts, key, rank, order, source, keep, last, filled):
    slots, row_tiles = key.shape[0], last.shape[0]
    count = counts[0, 0]

    @pl.loop(0, slots)
    def _(k):
        key[k] = jnp.where(k < count, rows[0, k], row_tiles) * slots + k

    @pl.loop(0, slots)
    def _(k):
        mine = key[k]
        rank[k] = sum((key[other] < mine).astype(jnp.int32) for other in range(slots))

    @pl.loop(0, slots)
    def _(n):
        slot = sum(jnp.where(rank[k] == n, k, 0) for k in range(slots))
        order[n] = slot
        source[n] = sources[0, slot]
        keep[n] = key[slot] // slots

    @pl.loop(0, row_tiles)
    def _(r):
        ahead = sum((key[k] < (r + 1) * slots).astype(jnp.int32) for k in range(slots))
        below = sum((key[k] < r * slots).astype(jnp.int32) for k in range(slots))
        last[r] = jnp.maximum(ahead - 1, 0)
        filled[r] = (ahead > below).astype(jnp.int32)


def kernel(
    times, slabs, refs,
    rows_hbm, sources_hbm, counts_hbm, lists_hbm, features, values_hbm, w_in_hbm, w_rec_hbm, bias_hbm,
    out,
    rows, sources, counts, lists, key, rank, order, source, keep, last_slot, filled,
    values, w_in, w_rec, bias, first0, first1, next0, next1, pack,
    arrived00, arrived01, arrived10, arrived11, sums, mixed, inputs, hidden, final, gates_even, gates_odd,
    small_sem, load_sem, slab_sem, ahead_sem, plane_sem, back_sem,
):
    time, slab = lax.axis_index("tm"), lax.axis_index("slab")
    slots, row_tiles = key.shape[0], last_slot.shape[0]
    tile = first0.shape[1]
    layers, _, width = w_in.shape
    units = width // 4
    halves = 2
    parts = [len(sizes) for sizes in CHUNKS]
    starts = [[times * sum(sizes[:n]) for n in range(len(sizes))] for sizes in CHUNKS]
    current = [[first0, first1], [next0, next1]]
    arrived = [[arrived00, arrived01], [arrived10, arrived11]]

    small = [
        pltpu.make_async_copy(a, b, small_sem.at[n])
        for n, (a, b) in enumerate(
            [(lists_hbm, lists), (rows_hbm, rows), (sources_hbm, sources), (counts_hbm, counts)]
        )
    ]
    loads = [
        pltpu.make_async_copy(a, b, load_sem.at[n])
        for n, (a, b) in enumerate(
            [
                (features.at[:, :, pl.ds(0, LANES)], first0),
                (features.at[:, :, pl.ds(LANES, LANES)], first1),
                (values_hbm, values),
                (w_in_hbm, w_in),
                (w_rec_hbm, w_rec),
                (bias_hbm, bias),
            ]
        )
    ]
    for load in small + loads:
        load.start()

    barrier = pltpu.get_barrier_semaphore()

    @pl.loop(1, slabs)
    def _(step):
        pl.semaphore_signal(barrier, device_id={"slab": lax.rem(slab + step, slabs)})

    @pl.loop(1, times)
    def _(step):
        pl.semaphore_signal(barrier, device_id={"tm": lax.rem(time + step, times)})

    small[0].wait()

    def pack_for(layer, half, q, target):
        for j in range(refs):
            target[j] = current[layer][half][lists[0, q, slab * refs + j]]

    def pack_all(layer, half):
        @pl.loop(1, slabs)
        def _(step):
            q = lax.rem(slab + step, slabs)
            pack_for(layer, half, q, pack.at[layer, half, q])

        pack_for(layer, half, slab, arrived[layer][half].at[pl.ds(slab * refs, refs)])

    def send_slab(layer, half):
        for step in range(1, slabs):
            q = lax.rem(slab + step, slabs)
            pltpu.make_async_remote_copy(
                src_ref=pack.at[layer, half, q],
                dst_ref=arrived[layer][half].at[pl.ds(slab * refs, refs)],
                send_sem=slab_sem.at[layer, half, 0],
                recv_sem=slab_sem.at[layer, half, 1],
                device_id={"slab": q},
            ).start()

    def slab_wait(layer, half, end):
        bulk_wait(pack.at[layer, half, pl.ds(0, slabs - 1)], slab_sem.at[layer, half, end])

    def add_slots(layer, half):
        total = jnp.zeros((tile, LANES), jnp.float32)
        for n in range(slots):
            product = jnp.dot(
                values[order[n]],
                arrived[layer][half][source[n]],
                preferred_element_type=jnp.float32,
            )
            if n > 0:
                same = (keep[n] == keep[n - 1]).astype(jnp.int32).astype(jnp.float32)
                product = total * same + product
            total = product
            sums[n] = total
        for r in range(row_tiles):
            live = filled[r].astype(jnp.float32)
            mixed[layer, half, r * tile : (r + 1) * tile, :] = (sums[last_slot[r]] * live).astype(
                jnp.bfloat16
            )

    def rows_of(layer, n, device):
        size, start = CHUNKS[layer][n], starts[layer][n]
        return pl.ds(pl.multiple_of(start + device * size, size), size)

    def every_peer(send):
        @pl.loop(1, times)
        def _(step):
            send(lax.rem(time + step, times))

    def far_first(send):
        send(lax.rem(time + times // 2, times))

        @pl.loop(1, times // 2)
        def _(step):
            send(lax.rem(time + times // 2 - step, times))
            send(lax.rem(time + times // 2 + step, times))

    def in_planes(half, n):
        return half == halves - 1 and n == 0

    def plane_wait(layer, m):
        size, start = CHUNKS[layer][0], starts[layer][0]
        near = time // BURST

        @pl.when(m != near)
        def _():
            bulk_wait(inputs.at[layer, halves - 1, pl.ds(start, BURST * size)], plane_sem.at[layer, m])

        @pl.when(m == near)
        def _():
            bulk_wait(
                inputs.at[layer, halves - 1, pl.ds(start, (BURST - 1) * size)], plane_sem.at[layer, m]
            )

    def send_ahead(layer, half, n):
        def send(peer):
            pltpu.make_async_remote_copy(
                src_ref=mixed.at[layer, half, rows_of(layer, n, peer)],
                dst_ref=inputs.at[layer, half, rows_of(layer, n, time)],
                send_sem=ahead_sem.at[layer, half, n, 0],
                recv_sem=(
                    plane_sem.at[layer, time // BURST]
                    if in_planes(half, n)
                    else ahead_sem.at[layer, half, n, 1]
                ),
                device_id={"tm": peer},
            ).start()

        return send

    def keep_own(layer, half, n):
        inputs[layer, half, rows_of(layer, n, time), :] = mixed[layer, half, rows_of(layer, n, time), :]

    def projected(layer, part):
        both = jnp.concatenate([inputs[layer, half, part, :] for half in range(halves)], axis=1)
        return (
            jnp.dot(both, w_in[layer], preferred_element_type=jnp.float32)
            + bias[layer : layer + 1, :]
        )

    def recur(layer, n, send=None):
        size = CHUNKS[layer][n]

        def advance(t, state, gate_inputs):
            before, memory = state
            part = rows_of(layer, n, t)
            total = gate_inputs + jnp.dot(
                before, w_rec[layer], preferred_element_type=jnp.float32
            )
            in_gate, forget, candidate, out_gate = (
                total[:, k * units : (k + 1) * units] for k in range(4)
            )
            memory = sigmoid(forget) * memory + sigmoid(in_gate) * jnp.tanh(candidate)
            after = (sigmoid(out_gate) * jnp.tanh(memory)).astype(jnp.bfloat16)
            if layer == layers - 1:
                final[part, :] = after
            else:
                for half in range(halves):
                    hidden[half, part, :] = after[:, half * LANES : (half + 1) * LANES]
            return after, memory

        def step(t, state):
            return advance(t, state, projected(layer, rows_of(layer, n, t)))

        zero = (jnp.zeros((size, units), jnp.bfloat16), jnp.zeros((size, units), jnp.float32))
        if n == 0:

            def plane(m, state):
                plane_wait(layer, m)
                for k in range(BURST):
                    state = step(m * BURST + k, state)
                return state

            lax.fori_loop(0, times // BURST, plane, zero)
            return

        if size <= SMALL and send is None:
            lax.fori_loop(0, times, step, zero, unroll=UNROLL)
            return

        bursts = times // BURST
        block = BURST * size

        def project(m, target):
            start = starts[layer][n] + jnp.minimum(m, bursts - 1) * block
            target[0:block, :] = projected(layer, pl.ds(pl.multiple_of(start, block), block))

        def burst(m, state, ready):
            for k in range(BURST):
                if size <= SMALL:
                    state = step(m * BURST + k, state)
                else:
                    state = advance(m * BURST + k, state, ready[k * size : (k + 1) * size, :])
            if send is not None:
                for k in range(1, BURST):
                    send(m * BURST + lax.rem(time + k, BURST))

                @pl.when(m != time // BURST)
                def _():
                    send(m * BURST + lax.rem(time, BURST))

            return state

        def two_bursts(m, state):
            for at, (ready, coming) in enumerate([(gates_even, gates_odd), (gates_odd, gates_even)]):
                if size > SMALL:
                    project(2 * m + at + 1, coming)
                state = burst(2 * m + at, state, ready)
            return state

        if size > SMALL:
            project(jnp.int32(0), gates_even)
        lax.fori_loop(0, bursts // 2, two_bursts, zero)

    def returned(layer, half):
        if layer == layers - 1:
            return final, out
        return hidden.at[half], current[layer + 1][half]

    def send_back(layer, half, n):
        kept, target = returned(layer, half)
        row = starts[layer][n] + time * CHUNKS[layer][n]
        place = pl.ds(pl.multiple_of(lax.rem(row, tile), CHUNKS[layer][n]), CHUNKS[layer][n])

        def send(peer):
            pltpu.make_async_remote_copy(
                src_ref=kept.at[rows_of(layer, n, peer)],
                dst_ref=target.at[row // tile, place],
                send_sem=back_sem.at[layer, half, n, 0],
                recv_sem=back_sem.at[layer, half, n, 1],
                device_id={"tm": peer},
            ).start()

        return send

    def return_own(layer, half, n):
        kept, target = returned(layer, half)
        row = starts[layer][n] + time * CHUNKS[layer][n]
        place = pl.ds(pl.multiple_of(lax.rem(row, tile), CHUNKS[layer][n]), CHUNKS[layer][n])
        target[row // tile, place, :] = kept[rows_of(layer, n, time), :]

    def peers_bytes(layer, n):
        return pl.ds(starts[layer][n], (times - 1) * CHUNKS[layer][n])

    loads[0].wait()
    pack_all(0, 0)
    pl.semaphore_wait(barrier, slabs - 1 + times - 1)

    for layer in range(layers):
        back_halves = range(1 if layer == layers - 1 else halves)
        final_part = parts[layer] - 1
        send_slab(layer, 0)
        if layer == 0:
            loads[1].wait()
        else:
            for n in range(parts[layer - 1]):
                bulk_wait(hidden.at[1, peers_bytes(layer - 1, n)], back_sem.at[layer - 1, 1, n, 1])
        pack_all(layer, 1)
        send_slab(layer, 1)
        if layer == 0:
            for load in small[1:]:
                load.wait()
            slot_table(
                rows, sources, counts, key, rank, order, source, keep, last_slot, filled
            )
            for load in loads[2:]:
                load.wait()

        for half in range(halves):
            slab_wait(layer, half, 1)
            add_slots(layer, half)
            for n in range(parts[layer]):
                (far_first if in_planes(half, n) else every_peer)(send_ahead(layer, half, n))
                keep_own(layer, half, n)

        for n in range(parts[layer]):
            for half in range(halves):
                if not in_planes(half, n):
                    bulk_wait(
                        inputs.at[layer, half, peers_bytes(layer, n)], ahead_sem.at[layer, half, n, 1]
                    )
            if n < final_part:
                recur(layer, n)
                for half in back_halves:
                    every_peer(send_back(layer, half, n))
            else:
                recur(layer, n, send_back(layer, 0, n))
            for half in back_halves:
                return_own(layer, half, n)

        if layer == layers - 1:
            for n in range(parts[layer]):
                bulk_wait(final.at[peers_bytes(layer, n)], back_sem.at[layer, 0, n, 1])
        else:
            bulk_wait(hidden.at[0, peers_bytes(layer, final_part)], back_sem.at[layer, 0, final_part, 0])
            every_peer(send_back(layer, 1, final_part))
            for n in range(parts[layer]):
                bulk_wait(hidden.at[0, peers_bytes(layer, n)], back_sem.at[layer, 0, n, 1])
            pack_all(layer + 1, 0)

    for layer in range(layers):
        for half in range(halves):
            slab_wait(layer, half, 0)
        for n in range(parts[layer]):
            for half in range(halves):
                bulk_wait(mixed.at[layer, half, peers_bytes(layer, n)], ahead_sem.at[layer, half, n, 0])
            if layer == layers - 1:
                bulk_wait(final.at[peers_bytes(layer, n)], back_sem.at[layer, 0, n, 0])
            else:
                for half in range(halves):
                    if n < parts[layer] - 1 or half > 0:
                        bulk_wait(hidden.at[half, peers_bytes(layer, n)], back_sem.at[layer, half, n, 0])


def pinned(x):
    return pltpu.with_memory_space_constraint(x, pltpu.HBM)


def local(
    features, ref_lists, tile_rows, tile_sources, tile_counts, tile_values, w_input, w_hidden, bias
):
    _, rows, width = features.shape
    _, slots, tile, _ = tile_values.shape
    layers, units = w_hidden.shape[:2]
    slabs, times = lax.axis_size("slab"), lax.axis_size("tm")
    refs = ref_lists.shape[2] // slabs
    row_tiles, listed, halves = rows // tile, slabs * refs, width // LANES
    parts = max(len(sizes) for sizes in CHUNKS)
    vmem = pl.BlockSpec(memory_space=pltpu.VMEM)
    far = pl.BlockSpec(memory_space=pltpu.HBM)
    narrow = pltpu.VMEM((row_tiles, tile, LANES), jnp.bfloat16)
    landing = pltpu.VMEM((listed, tile, LANES), jnp.bfloat16)
    half_rows = pltpu.VMEM((layers, halves, rows, LANES), jnp.bfloat16)
    result = pl.pallas_call(
        functools.partial(kernel, times, slabs, refs),
        out_shape=jax.ShapeDtypeStruct((row_tiles, tile, units), jnp.bfloat16),
        in_specs=[far] * 9,
        out_specs=vmem,
        scratch_shapes=[
            pltpu.SMEM(tile_rows.shape, jnp.int32),
            pltpu.SMEM(tile_sources.shape, jnp.int32),
            pltpu.SMEM(tile_counts.shape, jnp.int32),
            pltpu.SMEM(ref_lists.shape, jnp.int32),
            *[pltpu.SMEM((slots,), jnp.int32)] * 5,
            *[pltpu.SMEM((row_tiles,), jnp.int32)] * 2,
            pltpu.VMEM(tile_values.shape[1:], jnp.bfloat16),
            pltpu.VMEM(w_input.shape, jnp.bfloat16),
            pltpu.VMEM(w_hidden.shape, jnp.bfloat16),
            pltpu.VMEM(bias.shape, jnp.float32),
            *[narrow] * 4,
            pltpu.VMEM((layers, halves, slabs, refs, tile, LANES), jnp.bfloat16),
            *[landing] * 4,
            pltpu.VMEM((slots, tile, LANES), jnp.float32),
            half_rows,
            half_rows,
            pltpu.VMEM((halves, rows, LANES), jnp.bfloat16),
            pltpu.VMEM((rows, units), jnp.bfloat16),
            *[pltpu.VMEM((BURST * max(map(max, CHUNKS)), 4 * units), jnp.float32)] * 2,
            pltpu.SemaphoreType.DMA((4,)),
            pltpu.SemaphoreType.DMA((6,)),
            pltpu.SemaphoreType.DMA((layers, halves, 2)),
            pltpu.SemaphoreType.DMA((layers, halves, parts, 2)),
            pltpu.SemaphoreType.DMA((layers, times // BURST)),
            pltpu.SemaphoreType.DMA((layers, halves, parts, 2)),
        ],
        compiler_params=pltpu.CompilerParams(
            collective_id=0, has_side_effects=True, vmem_limit_bytes=48 << 20
        ),
    )(
        *map(pinned, (tile_rows, tile_sources)),
        tile_counts,
        *map(pinned, (ref_lists, features[0].reshape(row_tiles, tile, width), tile_values[0])),
        *map(pinned, (w_input, w_hidden, bias)),
    )
    return result.reshape(1, rows, units)


def solution(mesh):
    in_specs = (
        P("tm", "slab", None),
        P("tm", None, None),
        P("tm", "slab"),
        P("tm", "slab"),
        P("tm", "slab"),
        P("tm", "slab", None, None),
        P(),
        P(),
        P(),
    )
    out_specs = P("tm", "slab", None)
    return jax.shard_map(local, mesh=mesh, in_specs=in_specs, out_specs=out_specs, check_vma=False)
```

```python
import functools

import jax
import jax.numpy as jnp
from jax import lax
from jax.experimental import pallas as pl
from jax.experimental.pallas import tpu as pltpu
from jax.sharding import PartitionSpec as P

CHUNKS = ((16, 32), (16, 32))
BURST = 4
SMALL = 16
LANES = 128


def sigmoid(x):
    return 0.5 * jnp.tanh(0.5 * x) + 0.5


def bulk_wait(ref, sem):
    pltpu.make_async_copy(ref, ref, sem).wait()


def slot_table(rows, sources, counts, key, rank, order, source, keep, last, filled):
    slots, row_tiles = key.shape[0], last.shape[0]
    count = counts[0, 0]

    @pl.loop(0, slots)
    def _(k):
        key[k] = jnp.where(k < count, rows[0, k], row_tiles) * slots + k

    @pl.loop(0, slots)
    def _(k):
        mine = key[k]
        rank[k] = sum((key[other] < mine).astype(jnp.int32) for other in range(slots))

    @pl.loop(0, slots)
    def _(n):
        slot = sum(jnp.where(rank[k] == n, k, 0) for k in range(slots))
        order[n] = slot
        source[n] = sources[0, slot]
        keep[n] = key[slot] // slots

    @pl.loop(0, row_tiles)
    def _(r):
        ahead = sum((key[k] < (r + 1) * slots).astype(jnp.int32) for k in range(slots))
        below = sum((key[k] < r * slots).astype(jnp.int32) for k in range(slots))
        last[r] = jnp.maximum(ahead - 1, 0)
        filled[r] = (ahead > below).astype(jnp.int32)


def kernel(
    times, slabs, refs,
    rows_hbm, sources_hbm, counts_hbm, lists_hbm, features, values_hbm, w_in_hbm, w_rec_hbm, bias_hbm,
    out,
    rows, sources, counts, lists, key, rank, order, source, keep, last_slot, filled,
    values, w_in, w_rec, bias, first0, first1, next0, next1, pack,
    arrived00, arrived01, arrived10, arrived11, sums, mixed, inputs, hidden, final, gates_even, gates_odd,
    small_sem, load_sem, slab_sem, ahead_sem, plane_sem, back_sem,
):
    time, slab = lax.axis_index("tm"), lax.axis_index("slab")
    slots, row_tiles = key.shape[0], last_slot.shape[0]
    tile = first0.shape[1]
    layers, _, width = w_in.shape
    units = width // 4
    halves = 2
    parts = [len(sizes) for sizes in CHUNKS]
    starts = [[times * sum(sizes[:n]) for n in range(len(sizes))] for sizes in CHUNKS]
    current = [[first0, first1], [next0, next1]]
    arrived = [[arrived00, arrived01], [arrived10, arrived11]]

    small = [
        pltpu.make_async_copy(a, b, small_sem.at[n])
        for n, (a, b) in enumerate(
            [(lists_hbm, lists), (rows_hbm, rows), (sources_hbm, sources), (counts_hbm, counts)]
        )
    ]
    loads = [
        pltpu.make_async_copy(a, b, load_sem.at[n])
        for n, (a, b) in enumerate(
            [
                (features.at[:, :, pl.ds(0, LANES)], first0),
                (features.at[:, :, pl.ds(LANES, LANES)], first1),
                (values_hbm, values),
                (w_in_hbm, w_in),
                (w_rec_hbm, w_rec),
                (bias_hbm, bias),
            ]
        )
    ]
    for load in small + loads:
        load.start()

    barrier = pltpu.get_barrier_semaphore()

    @pl.loop(1, slabs)
    def _(step):
        pl.semaphore_signal(barrier, device_id={"slab": lax.rem(slab + step, slabs)})

    @pl.loop(1, times)
    def _(step):
        pl.semaphore_signal(barrier, device_id={"tm": lax.rem(time + step, times)})

    small[0].wait()

    def pack_for(layer, half, q, target):
        for j in range(refs):
            target[j] = current[layer][half][lists[0, q, slab * refs + j]]

    def pack_all(layer, half):
        @pl.loop(1, slabs)
        def _(step):
            q = lax.rem(slab + step, slabs)
            pack_for(layer, half, q, pack.at[layer, half, q])

        pack_for(layer, half, slab, arrived[layer][half].at[pl.ds(slab * refs, refs)])

    def send_slab(layer, half):
        for step in range(1, slabs):
            q = lax.rem(slab + step, slabs)
            pltpu.make_async_remote_copy(
                src_ref=pack.at[layer, half, q],
                dst_ref=arrived[layer][half].at[pl.ds(slab * refs, refs)],
                send_sem=slab_sem.at[layer, half, 0],
                recv_sem=slab_sem.at[layer, half, 1],
                device_id={"slab": q},
            ).start()

    def slab_wait(layer, half, end):
        bulk_wait(pack.at[layer, half, pl.ds(0, slabs - 1)], slab_sem.at[layer, half, end])

    def add_slots(layer, half):
        total = jnp.zeros((tile, LANES), jnp.float32)
        for n in range(slots):
            product = jnp.dot(
                values[order[n]],
                arrived[layer][half][source[n]],
                preferred_element_type=jnp.float32,
            )
            if n > 0:
                same = (keep[n] == keep[n - 1]).astype(jnp.int32).astype(jnp.float32)
                product = total * same + product
            total = product
            sums[n] = total
        for r in range(row_tiles):
            live = filled[r].astype(jnp.float32)
            mixed[layer, half, r * tile : (r + 1) * tile, :] = (sums[last_slot[r]] * live).astype(
                jnp.bfloat16
            )

    def rows_of(layer, n, device):
        size, start = CHUNKS[layer][n], starts[layer][n]
        return pl.ds(pl.multiple_of(start + device * size, size), size)

    def every_peer(send):
        @pl.loop(1, times)
        def _(step):
            send(lax.rem(time + step, times))

    def far_first(send):
        send(lax.rem(time + times // 2, times))

        @pl.loop(1, times // 2)
        def _(step):
            send(lax.rem(time + times // 2 - step, times))
            send(lax.rem(time + times // 2 + step, times))

    def in_planes(half, n):
        return half == halves - 1

    def plane_wait(layer, n, m):
        size, start = CHUNKS[layer][n], starts[layer][n]
        near = time // BURST

        @pl.when(m != near)
        def _():
            bulk_wait(
                inputs.at[layer, halves - 1, pl.ds(start, BURST * size)], plane_sem.at[layer, n, m]
            )

        @pl.when(m == near)
        def _():
            bulk_wait(
                inputs.at[layer, halves - 1, pl.ds(start, (BURST - 1) * size)], plane_sem.at[layer, n, m]
            )

    def send_ahead(layer, half, n):
        def send(peer):
            pltpu.make_async_remote_copy(
                src_ref=mixed.at[layer, half, rows_of(layer, n, peer)],
                dst_ref=inputs.at[layer, half, rows_of(layer, n, time)],
                send_sem=ahead_sem.at[layer, half, n, 0],
                recv_sem=(
                    plane_sem.at[layer, n, time // BURST]
                    if in_planes(half, n)
                    else ahead_sem.at[layer, half, n, 1]
                ),
                device_id={"tm": peer},
            ).start()

        return send

    def keep_own(layer, half, n):
        inputs[layer, half, rows_of(layer, n, time), :] = mixed[layer, half, rows_of(layer, n, time), :]

    def projected(layer, part):
        both = jnp.concatenate([inputs[layer, half, part, :] for half in range(halves)], axis=1)
        return (
            jnp.dot(both, w_in[layer], preferred_element_type=jnp.float32)
            + bias[layer : layer + 1, :]
        )

    def recur(layer, n, send=None):
        size = CHUNKS[layer][n]

        def advance(t, state, gate_inputs):
            before, memory = state
            part = rows_of(layer, n, t)
            total = gate_inputs + jnp.dot(
                before, w_rec[layer], preferred_element_type=jnp.float32
            )
            in_gate, forget, candidate, out_gate = (
                total[:, k * units : (k + 1) * units] for k in range(4)
            )
            memory = sigmoid(forget) * memory + sigmoid(in_gate) * jnp.tanh(candidate)
            after = (sigmoid(out_gate) * jnp.tanh(memory)).astype(jnp.bfloat16)
            if layer == layers - 1:
                final[part, :] = after
            else:
                for half in range(halves):
                    hidden[half, part, :] = after[:, half * LANES : (half + 1) * LANES]
            return after, memory

        def step(t, state):
            return advance(t, state, projected(layer, rows_of(layer, n, t)))

        zero = (jnp.zeros((size, units), jnp.bfloat16), jnp.zeros((size, units), jnp.float32))
        if size <= SMALL and send is None:

            def plane(m, state):
                plane_wait(layer, n, m)
                for k in range(BURST):
                    state = step(m * BURST + k, state)
                return state

            lax.fori_loop(0, times // BURST, plane, zero)
            return

        bursts = times // BURST
        block = BURST * size

        def project(m, target):
            start = starts[layer][n] + jnp.minimum(m, bursts - 1) * block
            pl.when(m < bursts)(lambda: plane_wait(layer, n, m))
            target[0:block, :] = projected(layer, pl.ds(pl.multiple_of(start, block), block))

        def burst(m, state, ready):
            if size <= SMALL:
                plane_wait(layer, n, m)
            for k in range(BURST):
                if size <= SMALL:
                    state = step(m * BURST + k, state)
                else:
                    state = advance(m * BURST + k, state, ready[k * size : (k + 1) * size, :])
            if send is not None:
                for k in range(1, BURST):
                    send(m * BURST + lax.rem(time + k, BURST))

                @pl.when(m != time // BURST)
                def _():
                    send(m * BURST + lax.rem(time, BURST))

            return state

        def two_bursts(m, state):
            for at, (ready, coming) in enumerate([(gates_even, gates_odd), (gates_odd, gates_even)]):
                if size > SMALL:
                    project(2 * m + at + 1, coming)
                state = burst(2 * m + at, state, ready)
            return state

        if size > SMALL:
            project(jnp.int32(0), gates_even)
        lax.fori_loop(0, bursts // 2, two_bursts, zero)

    def returned(layer, half):
        if layer == layers - 1:
            return final, out
        return hidden.at[half], current[layer + 1][half]

    def send_back(layer, half, n):
        kept, target = returned(layer, half)
        row = starts[layer][n] + time * CHUNKS[layer][n]
        place = pl.ds(pl.multiple_of(lax.rem(row, tile), CHUNKS[layer][n]), CHUNKS[layer][n])

        def send(peer):
            pltpu.make_async_remote_copy(
                src_ref=kept.at[rows_of(layer, n, peer)],
                dst_ref=target.at[row // tile, place],
                send_sem=back_sem.at[layer, half, n, 0],
                recv_sem=back_sem.at[layer, half, n, 1],
                device_id={"tm": peer},
            ).start()

        return send

    def return_own(layer, half, n):
        kept, target = returned(layer, half)
        row = starts[layer][n] + time * CHUNKS[layer][n]
        place = pl.ds(pl.multiple_of(lax.rem(row, tile), CHUNKS[layer][n]), CHUNKS[layer][n])
        target[row // tile, place, :] = kept[rows_of(layer, n, time), :]

    def peers_bytes(layer, n):
        return pl.ds(starts[layer][n], (times - 1) * CHUNKS[layer][n])

    loads[0].wait()
    pack_all(0, 0)
    pl.semaphore_wait(barrier, slabs - 1 + times - 1)

    for layer in range(layers):
        back_halves = range(1 if layer == layers - 1 else halves)
        final_part = parts[layer] - 1
        send_slab(layer, 0)
        if layer == 0:
            loads[1].wait()
        else:
            for n in range(parts[layer - 1]):
                bulk_wait(hidden.at[1, peers_bytes(layer - 1, n)], back_sem.at[layer - 1, 1, n, 1])
        pack_all(layer, 1)
        send_slab(layer, 1)
        if layer == 0:
            for load in small[1:]:
                load.wait()
            slot_table(
                rows, sources, counts, key, rank, order, source, keep, last_slot, filled
            )
            for load in loads[2:]:
                load.wait()

        for half in range(halves):
            slab_wait(layer, half, 1)
            add_slots(layer, half)
            for n in range(parts[layer]):
                (far_first if in_planes(half, n) else every_peer)(send_ahead(layer, half, n))
                keep_own(layer, half, n)

        for n in range(parts[layer]):
            for half in range(halves):
                if not in_planes(half, n):
                    bulk_wait(
                        inputs.at[layer, half, peers_bytes(layer, n)], ahead_sem.at[layer, half, n, 1]
                    )
            if n < final_part:
                recur(layer, n)
                for half in back_halves:
                    every_peer(send_back(layer, half, n))
            else:
                recur(layer, n, send_back(layer, 0, n))
            for half in back_halves:
                return_own(layer, half, n)

        if layer == layers - 1:
            for n in range(parts[layer]):
                bulk_wait(final.at[peers_bytes(layer, n)], back_sem.at[layer, 0, n, 1])
        else:
            bulk_wait(hidden.at[0, peers_bytes(layer, final_part)], back_sem.at[layer, 0, final_part, 0])
            every_peer(send_back(layer, 1, final_part))
            for n in range(parts[layer]):
                bulk_wait(hidden.at[0, peers_bytes(layer, n)], back_sem.at[layer, 0, n, 1])
            pack_all(layer + 1, 0)

    for layer in range(layers):
        for half in range(halves):
            slab_wait(layer, half, 0)
        for n in range(parts[layer]):
            for half in range(halves):
                bulk_wait(mixed.at[layer, half, peers_bytes(layer, n)], ahead_sem.at[layer, half, n, 0])
            if layer == layers - 1:
                bulk_wait(final.at[peers_bytes(layer, n)], back_sem.at[layer, 0, n, 0])
            else:
                for half in range(halves):
                    if n < parts[layer] - 1 or half > 0:
                        bulk_wait(hidden.at[half, peers_bytes(layer, n)], back_sem.at[layer, half, n, 0])


def pinned(x):
    return pltpu.with_memory_space_constraint(x, pltpu.HBM)


def local(
    features, ref_lists, tile_rows, tile_sources, tile_counts, tile_values, w_input, w_hidden, bias
):
    _, rows, width = features.shape
    _, slots, tile, _ = tile_values.shape
    layers, units = w_hidden.shape[:2]
    slabs, times = lax.axis_size("slab"), lax.axis_size("tm")
    refs = ref_lists.shape[2] // slabs
    row_tiles, listed, halves = rows // tile, slabs * refs, width // LANES
    parts = max(len(sizes) for sizes in CHUNKS)
    vmem = pl.BlockSpec(memory_space=pltpu.VMEM)
    far = pl.BlockSpec(memory_space=pltpu.HBM)
    narrow = pltpu.VMEM((row_tiles, tile, LANES), jnp.bfloat16)
    landing = pltpu.VMEM((listed, tile, LANES), jnp.bfloat16)
    half_rows = pltpu.VMEM((layers, halves, rows, LANES), jnp.bfloat16)
    result = pl.pallas_call(
        functools.partial(kernel, times, slabs, refs),
        out_shape=jax.ShapeDtypeStruct((row_tiles, tile, units), jnp.bfloat16),
        in_specs=[far] * 9,
        out_specs=vmem,
        scratch_shapes=[
            pltpu.SMEM(tile_rows.shape, jnp.int32),
            pltpu.SMEM(tile_sources.shape, jnp.int32),
            pltpu.SMEM(tile_counts.shape, jnp.int32),
            pltpu.SMEM(ref_lists.shape, jnp.int32),
            *[pltpu.SMEM((slots,), jnp.int32)] * 5,
            *[pltpu.SMEM((row_tiles,), jnp.int32)] * 2,
            pltpu.VMEM(tile_values.shape[1:], jnp.bfloat16),
            pltpu.VMEM(w_input.shape, jnp.bfloat16),
            pltpu.VMEM(w_hidden.shape, jnp.bfloat16),
            pltpu.VMEM(bias.shape, jnp.float32),
            *[narrow] * 4,
            pltpu.VMEM((layers, halves, slabs, refs, tile, LANES), jnp.bfloat16),
            *[landing] * 4,
            pltpu.VMEM((slots, tile, LANES), jnp.float32),
            half_rows,
            half_rows,
            pltpu.VMEM((halves, rows, LANES), jnp.bfloat16),
            pltpu.VMEM((rows, units), jnp.bfloat16),
            *[pltpu.VMEM((BURST * max(map(max, CHUNKS)), 4 * units), jnp.float32)] * 2,
            pltpu.SemaphoreType.DMA((4,)),
            pltpu.SemaphoreType.DMA((6,)),
            pltpu.SemaphoreType.DMA((layers, halves, 2)),
            pltpu.SemaphoreType.DMA((layers, halves, parts, 2)),
            pltpu.SemaphoreType.DMA((layers, parts, times // BURST)),
            pltpu.SemaphoreType.DMA((layers, halves, parts, 2)),
        ],
        compiler_params=pltpu.CompilerParams(
            collective_id=0, has_side_effects=True, vmem_limit_bytes=48 << 20
        ),
    )(
        *map(pinned, (tile_rows, tile_sources)),
        tile_counts,
        *map(pinned, (ref_lists, features[0].reshape(row_tiles, tile, width), tile_values[0])),
        *map(pinned, (w_input, w_hidden, bias)),
    )
    return result.reshape(1, rows, units)


def solution(mesh):
    in_specs = (
        P("tm", "slab", None),
        P("tm", None, None),
        P("tm", "slab"),
        P("tm", "slab"),
        P("tm", "slab"),
        P("tm", "slab", None, None),
        P(),
        P(),
        P(),
    )
    out_specs = P("tm", "slab", None)
    return jax.shard_map(local, mesh=mesh, in_specs=in_specs, out_specs=out_specs, check_vma=False)
```

```python
import functools

import jax
import jax.numpy as jnp
from jax import lax
from jax.experimental import pallas as pl
from jax.experimental.pallas import tpu as pltpu
from jax.sharding import PartitionSpec as P

CHUNKS = ((16, 32), (16, 32))
BURST = 4
SMALL = 16
LANES = 128


def sigmoid(x):
    return 0.5 * jnp.tanh(0.5 * x) + 0.5


def bulk_wait(ref, sem):
    pltpu.make_async_copy(ref, ref, sem).wait()


def slot_table(rows, sources, counts, key, rank, order, source, keep, last, filled):
    slots, row_tiles = key.shape[0], last.shape[0]
    count = counts[0, 0]

    @pl.loop(0, slots)
    def _(k):
        key[k] = jnp.where(k < count, rows[0, k], row_tiles) * slots + k

    @pl.loop(0, slots)
    def _(k):
        mine = key[k]
        rank[k] = sum((key[other] < mine).astype(jnp.int32) for other in range(slots))

    @pl.loop(0, slots)
    def _(n):
        slot = sum(jnp.where(rank[k] == n, k, 0) for k in range(slots))
        order[n] = slot
        source[n] = sources[0, slot]
        keep[n] = key[slot] // slots

    @pl.loop(0, row_tiles)
    def _(r):
        ahead = sum((key[k] < (r + 1) * slots).astype(jnp.int32) for k in range(slots))
        below = sum((key[k] < r * slots).astype(jnp.int32) for k in range(slots))
        last[r] = jnp.maximum(ahead - 1, 0)
        filled[r] = (ahead > below).astype(jnp.int32)


def kernel(
    times, slabs, refs,
    rows_hbm, sources_hbm, counts_hbm, lists_hbm, features, values_hbm, w_in_hbm, w_rec_hbm, bias_hbm,
    out,
    rows, sources, counts, lists, key, rank, order, source, keep, last_slot, filled,
    values, w_in, w_rec, bias, first0, first1, next0, next1, pack,
    arrived00, arrived01, arrived10, arrived11, sums, mixed, inputs, hidden, final, gates_even, gates_odd,
    small_sem, load_sem, slab_sem, ahead_sem, plane_sem, back_sem,
):
    time, slab = lax.axis_index("tm"), lax.axis_index("slab")
    slots, row_tiles = key.shape[0], last_slot.shape[0]
    tile = first0.shape[1]
    layers, _, width = w_in.shape
    units = width // 4
    halves = 2
    parts = [len(sizes) for sizes in CHUNKS]
    starts = [[times * sum(sizes[:n]) for n in range(len(sizes))] for sizes in CHUNKS]
    current = [[first0, first1], [next0, next1]]
    arrived = [[arrived00, arrived01], [arrived10, arrived11]]

    small = [
        pltpu.make_async_copy(a, b, small_sem.at[n])
        for n, (a, b) in enumerate(
            [(lists_hbm, lists), (rows_hbm, rows), (sources_hbm, sources), (counts_hbm, counts)]
        )
    ]
    loads = [
        pltpu.make_async_copy(a, b, load_sem.at[n])
        for n, (a, b) in enumerate(
            [
                (features.at[:, :, pl.ds(0, LANES)], first0),
                (features.at[:, :, pl.ds(LANES, LANES)], first1),
                (values_hbm, values),
                (w_in_hbm, w_in),
                (w_rec_hbm, w_rec),
                (bias_hbm, bias),
            ]
        )
    ]
    for load in small + loads:
        load.start()

    barrier = pltpu.get_barrier_semaphore()

    @pl.loop(1, slabs)
    def _(step):
        pl.semaphore_signal(barrier, device_id={"slab": lax.rem(slab + step, slabs)})

    @pl.loop(1, times)
    def _(step):
        pl.semaphore_signal(barrier, device_id={"tm": lax.rem(time + step, times)})

    small[0].wait()

    def pack_for(layer, half, q, target):
        for j in range(refs):
            target[j] = current[layer][half][lists[0, q, slab * refs + j]]

    def pack_all(layer, half):
        @pl.loop(1, slabs)
        def _(step):
            q = lax.rem(slab + step, slabs)
            pack_for(layer, half, q, pack.at[layer, half, q])

        pack_for(layer, half, slab, arrived[layer][half].at[pl.ds(slab * refs, refs)])

    def send_slab(layer, half):
        for step in range(1, slabs):
            q = lax.rem(slab + step, slabs)
            pltpu.make_async_remote_copy(
                src_ref=pack.at[layer, half, q],
                dst_ref=arrived[layer][half].at[pl.ds(slab * refs, refs)],
                send_sem=slab_sem.at[layer, half, 0],
                recv_sem=slab_sem.at[layer, half, 1],
                device_id={"slab": q},
            ).start()

    def slab_wait(layer, half, end):
        bulk_wait(pack.at[layer, half, pl.ds(0, slabs - 1)], slab_sem.at[layer, half, end])

    def add_slots(layer, half):
        total = jnp.zeros((tile, LANES), jnp.float32)
        for n in range(slots):
            product = jnp.dot(
                values[order[n]],
                arrived[layer][half][source[n]],
                preferred_element_type=jnp.float32,
            )
            if n > 0:
                same = (keep[n] == keep[n - 1]).astype(jnp.int32).astype(jnp.float32)
                product = total * same + product
            total = product
            sums[n] = total
        for r in range(row_tiles):
            live = filled[r].astype(jnp.float32)
            mixed[layer, half, r * tile : (r + 1) * tile, :] = (sums[last_slot[r]] * live).astype(
                jnp.bfloat16
            )

    def rows_of(layer, n, device):
        size, start = CHUNKS[layer][n], starts[layer][n]
        return pl.ds(pl.multiple_of(start + device * size, size), size)

    def every_peer(send):
        @pl.loop(1, times)
        def _(step):
            send(lax.rem(time + step, times))

    def far_first(send):
        send(lax.rem(time + times // 2, times))

        @pl.loop(1, times // 2)
        def _(step):
            send(lax.rem(time + times // 2 - step, times))
            send(lax.rem(time + times // 2 + step, times))

    def in_planes(half, n):
        return half == halves - 1

    def plane_wait(layer, n, m):
        size, start = CHUNKS[layer][n], starts[layer][n]
        near = time // BURST

        @pl.when(m != near)
        def _():
            bulk_wait(
                inputs.at[layer, halves - 1, pl.ds(start, BURST * size)], plane_sem.at[layer, n, m]
            )

        @pl.when(m == near)
        def _():
            bulk_wait(
                inputs.at[layer, halves - 1, pl.ds(start, (BURST - 1) * size)], plane_sem.at[layer, n, m]
            )

    def send_ahead(layer, half, n):
        def send(peer):
            pltpu.make_async_remote_copy(
                src_ref=mixed.at[layer, half, rows_of(layer, n, peer)],
                dst_ref=inputs.at[layer, half, rows_of(layer, n, time)],
                send_sem=ahead_sem.at[layer, half, n, 0],
                recv_sem=(
                    plane_sem.at[layer, n, time // BURST]
                    if in_planes(half, n)
                    else ahead_sem.at[layer, half, n, 1]
                ),
                device_id={"tm": peer},
            ).start()

        return send

    def keep_own(layer, half, n):
        inputs[layer, half, rows_of(layer, n, time), :] = mixed[layer, half, rows_of(layer, n, time), :]

    def projected(layer, part):
        both = jnp.concatenate([inputs[layer, half, part, :] for half in range(halves)], axis=1)
        return (
            jnp.dot(both, w_in[layer], preferred_element_type=jnp.float32)
            + bias[layer : layer + 1, :]
        )

    def recur(layer, n, send=None):
        size = CHUNKS[layer][n]

        def advance(t, state, gate_inputs):
            before, memory = state
            part = rows_of(layer, n, t)
            total = gate_inputs + jnp.dot(
                before, w_rec[layer], preferred_element_type=jnp.float32
            )
            in_gate, forget, candidate, out_gate = (
                total[:, k * units : (k + 1) * units] for k in range(4)
            )
            memory = sigmoid(forget) * memory + sigmoid(in_gate) * jnp.tanh(candidate)
            after = (sigmoid(out_gate) * jnp.tanh(memory)).astype(jnp.bfloat16)
            if layer == layers - 1:
                final[part, :] = after
            else:
                for half in range(halves):
                    hidden[half, part, :] = after[:, half * LANES : (half + 1) * LANES]
            return after, memory

        def step(t, state):
            return advance(t, state, projected(layer, rows_of(layer, n, t)))

        zero = (jnp.zeros((size, units), jnp.bfloat16), jnp.zeros((size, units), jnp.float32))
        if size <= SMALL and send is None:

            def plane(m, state):
                plane_wait(layer, n, m)
                for k in range(BURST):
                    state = step(m * BURST + k, state)
                return state

            lax.fori_loop(0, times // BURST, plane, zero)
            return

        bursts = times // BURST
        block = BURST * size

        def project(m, target):
            start = starts[layer][n] + jnp.minimum(m, bursts - 1) * block
            pl.when(m < bursts)(lambda: plane_wait(layer, n, m))
            target[0:block, :] = projected(layer, pl.ds(pl.multiple_of(start, block), block))

        def burst(m, state, ready):
            if size <= SMALL:
                plane_wait(layer, n, m)
            for k in range(BURST):
                if size <= SMALL:
                    state = step(m * BURST + k, state)
                else:
                    state = advance(m * BURST + k, state, ready[k * size : (k + 1) * size, :])
            if send is not None:
                for k in range(1, BURST):
                    send(m * BURST + lax.rem(time + k, BURST))

                @pl.when(m != time // BURST)
                def _():
                    send(m * BURST + lax.rem(time, BURST))

            return state

        def two_bursts(m, state):
            for at, (ready, coming) in enumerate([(gates_even, gates_odd), (gates_odd, gates_even)]):
                if size > SMALL:
                    project(2 * m + at + 1, coming)
                state = burst(2 * m + at, state, ready)
            return state

        if size > SMALL:
            project(jnp.int32(0), gates_even)
        lax.fori_loop(0, bursts // 2, two_bursts, zero)

    def returned(layer, half):
        if layer == layers - 1:
            return final, out
        return hidden.at[half], current[layer + 1][half]

    def send_back(layer, half, n):
        kept, target = returned(layer, half)
        row = starts[layer][n] + time * CHUNKS[layer][n]
        place = pl.ds(pl.multiple_of(lax.rem(row, tile), CHUNKS[layer][n]), CHUNKS[layer][n])

        def send(peer):
            pltpu.make_async_remote_copy(
                src_ref=kept.at[rows_of(layer, n, peer)],
                dst_ref=target.at[row // tile, place],
                send_sem=back_sem.at[layer, half, n, 0],
                recv_sem=back_sem.at[layer, half, n, 1],
                device_id={"tm": peer},
            ).start()

        return send

    def return_own(layer, half, n):
        kept, target = returned(layer, half)
        row = starts[layer][n] + time * CHUNKS[layer][n]
        place = pl.ds(pl.multiple_of(lax.rem(row, tile), CHUNKS[layer][n]), CHUNKS[layer][n])
        target[row // tile, place, :] = kept[rows_of(layer, n, time), :]

    def peers_bytes(layer, n):
        return pl.ds(starts[layer][n], (times - 1) * CHUNKS[layer][n])

    loads[0].wait()
    pack_all(0, 0)
    pl.semaphore_wait(barrier, slabs - 1 + times - 1)

    for layer in range(layers):
        back_halves = range(1 if layer == layers - 1 else halves)
        final_part = parts[layer] - 1
        send_slab(layer, 0)
        if layer == 0:
            loads[1].wait()
        else:
            for n in range(parts[layer - 1]):
                bulk_wait(hidden.at[1, peers_bytes(layer - 1, n)], back_sem.at[layer - 1, 1, n, 1])
        pack_all(layer, 1)
        send_slab(layer, 1)
        if layer == 0:
            for load in small[1:]:
                load.wait()
            slot_table(
                rows, sources, counts, key, rank, order, source, keep, last_slot, filled
            )
            for load in loads[2:]:
                load.wait()

        for half in range(halves):
            slab_wait(layer, half, 1)
            add_slots(layer, half)
            for n in range(parts[layer]):
                (far_first if in_planes(half, n) else every_peer)(send_ahead(layer, half, n))
                keep_own(layer, half, n)

        for n in range(parts[layer]):
            for half in range(halves):
                if not in_planes(half, n):
                    bulk_wait(
                        inputs.at[layer, half, peers_bytes(layer, n)], ahead_sem.at[layer, half, n, 1]
                    )
            if n < final_part and layer < layers - 1:
                recur(layer, n)
                for half in back_halves:
                    every_peer(send_back(layer, half, n))
            else:
                recur(layer, n, send_back(layer, 0, n))
            for half in back_halves:
                return_own(layer, half, n)

        if layer == layers - 1:
            for n in range(parts[layer]):
                bulk_wait(final.at[peers_bytes(layer, n)], back_sem.at[layer, 0, n, 1])
        else:
            bulk_wait(hidden.at[0, peers_bytes(layer, final_part)], back_sem.at[layer, 0, final_part, 0])
            every_peer(send_back(layer, 1, final_part))
            for n in range(parts[layer]):
                bulk_wait(hidden.at[0, peers_bytes(layer, n)], back_sem.at[layer, 0, n, 1])
            pack_all(layer + 1, 0)

    for layer in range(layers):
        for half in range(halves):
            slab_wait(layer, half, 0)
        for n in range(parts[layer]):
            for half in range(halves):
                bulk_wait(mixed.at[layer, half, peers_bytes(layer, n)], ahead_sem.at[layer, half, n, 0])
            if layer == layers - 1:
                bulk_wait(final.at[peers_bytes(layer, n)], back_sem.at[layer, 0, n, 0])
            else:
                for half in range(halves):
                    if n < parts[layer] - 1 or half > 0:
                        bulk_wait(hidden.at[half, peers_bytes(layer, n)], back_sem.at[layer, half, n, 0])


def pinned(x):
    return pltpu.with_memory_space_constraint(x, pltpu.HBM)


def local(
    features, ref_lists, tile_rows, tile_sources, tile_counts, tile_values, w_input, w_hidden, bias
):
    _, rows, width = features.shape
    _, slots, tile, _ = tile_values.shape
    layers, units = w_hidden.shape[:2]
    slabs, times = lax.axis_size("slab"), lax.axis_size("tm")
    refs = ref_lists.shape[2] // slabs
    row_tiles, listed, halves = rows // tile, slabs * refs, width // LANES
    parts = max(len(sizes) for sizes in CHUNKS)
    vmem = pl.BlockSpec(memory_space=pltpu.VMEM)
    far = pl.BlockSpec(memory_space=pltpu.HBM)
    narrow = pltpu.VMEM((row_tiles, tile, LANES), jnp.bfloat16)
    landing = pltpu.VMEM((listed, tile, LANES), jnp.bfloat16)
    half_rows = pltpu.VMEM((layers, halves, rows, LANES), jnp.bfloat16)
    result = pl.pallas_call(
        functools.partial(kernel, times, slabs, refs),
        out_shape=jax.ShapeDtypeStruct((row_tiles, tile, units), jnp.bfloat16),
        in_specs=[far] * 9,
        out_specs=vmem,
        scratch_shapes=[
            pltpu.SMEM(tile_rows.shape, jnp.int32),
            pltpu.SMEM(tile_sources.shape, jnp.int32),
            pltpu.SMEM(tile_counts.shape, jnp.int32),
            pltpu.SMEM(ref_lists.shape, jnp.int32),
            *[pltpu.SMEM((slots,), jnp.int32)] * 5,
            *[pltpu.SMEM((row_tiles,), jnp.int32)] * 2,
            pltpu.VMEM(tile_values.shape[1:], jnp.bfloat16),
            pltpu.VMEM(w_input.shape, jnp.bfloat16),
            pltpu.VMEM(w_hidden.shape, jnp.bfloat16),
            pltpu.VMEM(bias.shape, jnp.float32),
            *[narrow] * 4,
            pltpu.VMEM((layers, halves, slabs, refs, tile, LANES), jnp.bfloat16),
            *[landing] * 4,
            pltpu.VMEM((slots, tile, LANES), jnp.float32),
            half_rows,
            half_rows,
            pltpu.VMEM((halves, rows, LANES), jnp.bfloat16),
            pltpu.VMEM((rows, units), jnp.bfloat16),
            *[pltpu.VMEM((BURST * max(map(max, CHUNKS)), 4 * units), jnp.float32)] * 2,
            pltpu.SemaphoreType.DMA((4,)),
            pltpu.SemaphoreType.DMA((6,)),
            pltpu.SemaphoreType.DMA((layers, halves, 2)),
            pltpu.SemaphoreType.DMA((layers, halves, parts, 2)),
            pltpu.SemaphoreType.DMA((layers, parts, times // BURST)),
            pltpu.SemaphoreType.DMA((layers, halves, parts, 2)),
        ],
        compiler_params=pltpu.CompilerParams(
            collective_id=0, has_side_effects=True, vmem_limit_bytes=48 << 20
        ),
    )(
        *map(pinned, (tile_rows, tile_sources)),
        tile_counts,
        *map(pinned, (ref_lists, features[0].reshape(row_tiles, tile, width), tile_values[0])),
        *map(pinned, (w_input, w_hidden, bias)),
    )
    return result.reshape(1, rows, units)


def solution(mesh):
    in_specs = (
        P("tm", "slab", None),
        P("tm", None, None),
        P("tm", "slab"),
        P("tm", "slab"),
        P("tm", "slab"),
        P("tm", "slab", None, None),
        P(),
        P(),
        P(),
    )
    out_specs = P("tm", "slab", None)
    return jax.shard_map(local, mesh=mesh, in_specs=in_specs, out_specs=out_specs, check_vma=False)
```
